32 devices in a mesh: group: 4 (over x, core), dev: 8 (over z, y).
Axes of the slice: x: 2, y: 2, z: 4, core: 2. Of those that a mesh axis runs over, the one named last changes fastest.
Arguments:
- images: bfloat16 [4096, 1152], P(('group', 'dev')), may hold values from -1 to 1
- texts: bfloat16 [4096, 1152], P(('group', 'dev')), may hold values from -1 to 1
- lang_order: int32 [4096], P(('group', 'dev')), may hold values from 0 to 1023, as said below
- position: int32 [4096], P(('group', 'dev')), may hold values from 0 to 1023, as said below
- logit_scale: float32 [1], replicated, may hold values from 8 to 24
- logit_bias: float32 [1], replicated, may hold values from -4 to -1
Outputs:
- image_grad: float32 [4096, 1152], P(('group', 'dev'))
- text_grad: float32 [4096, 1152], P(('group', 'dev'))
- loss: float32 [1], replicated
The draws below stay inside these ranges and needn't reach their ends.
Inputs may be any that keep to these rules, and one draw needn't show every extreme that they name: In each group of 1024 examples, lang_order is a permutation of the group-local indices; the 128 entries of one device name at most 16 examples held by any one device of the group, and exactly 16 for each device they name. position is the inverse of lang_order within each group.
All inputs are finite; a program needn't handle non-finite values.
Results may differ from the reference program's by a relative error of at most 0.00062.
Values may be sent and summed in bfloat16 or wider, within the bound.
No kernel may reach another device: no remote copies, remote signals or barrier semaphores. Data moves between devices by JAX's collectives and lax.ppermute only.
A program may use at most 64 MiB of HBM per device.

```python
import math
import jax
import jax.numpy as jnp
from jax import lax

D = 1152
ROWS = 128
N_GROUP = 4
N_DEV = 8


def lang_maps(key):
    group_count = N_GROUP
    dev_count = N_DEV
    row_count = ROWS
    slot_depth = ROWS // 8
    per_source = row_count // slot_depth
    key_list = jax.random.split(jax.random.fold_in(key, 7), 4)
    shifts = jax.vmap(lambda subkey: jax.random.permutation(subkey, dev_count)[:per_source])(jax.random.split(key_list[0], group_count))
    relabel = jax.vmap(lambda subkey: jax.random.permutation(subkey, dev_count))(jax.random.split(key_list[1], group_count))
    within = jax.vmap(lambda subkey: jax.random.permutation(subkey, per_source))(jax.random.split(key_list[2], group_count * dev_count)).reshape(group_count, dev_count, per_source)
    scramble = jax.vmap(lambda subkey: jax.random.permutation(subkey, row_count))(jax.random.split(key_list[3], group_count * dev_count)).reshape(group_count, dev_count, row_count)
    span = dev_count * row_count
    place_ids = jnp.arange(span, dtype=jnp.int32)
    source = place_ids // row_count
    which = place_ids % row_count // slot_depth
    offset = place_ids % slot_depth
    group_ids = jnp.arange(group_count, dtype=jnp.int32)[:, None]
    pick = within[group_ids, source[None, :], which[None, :]]
    target_dev = (relabel[group_ids, source[None, :]] + jnp.take_along_axis(shifts, pick, axis=1)) % dev_count
    local = scramble[group_ids, target_dev, pick * slot_depth + offset[None, :]]
    ordering = (target_dev * row_count + local).astype(jnp.int32)
    inverse = jnp.zeros_like(ordering).at[group_ids, ordering].set(jnp.broadcast_to(place_ids[None, :], (group_count, span)))
    return (ordering.reshape(-1).astype(jnp.int32), inverse.reshape(-1).astype(jnp.int32))


def embed_parts(key):
    total = N_GROUP * N_DEV * ROWS
    mix_count = 8
    key_list = jax.random.split(jax.random.fold_in(key, 11), 7)
    root = jnp.float32(D) ** (-0.5)
    directions = jax.random.normal(key_list[0], (mix_count, D), jnp.float32) * root
    weights = jax.random.normal(key_list[1], (total, mix_count), jnp.float32) * jnp.float32(mix_count) ** (-0.5)
    cluster = jnp.dot(weights, directions, precision=jax.lax.Precision.HIGHEST)
    shared = jax.random.normal(key_list[2], (total, D), jnp.float32) * root
    img_noise = jax.random.normal(key_list[3], (total, D), jnp.float32) * root
    txt_noise = jax.random.normal(key_list[4], (total, D), jnp.float32) * root
    img_scale = jnp.exp(jax.random.uniform(key_list[5], (total, 1), jnp.float32, -0.6931472, 0.6931472))
    txt_scale = jnp.exp(jax.random.uniform(key_list[6], (total, 1), jnp.float32, -0.6931472, 0.6931472))
    cluster_weight = 0.63
    image_rows = (cluster_weight * cluster + 0.5 * shared + 0.6 * img_noise) * img_scale
    text_rows = (cluster_weight * cluster + 0.5 * shared + 0.6 * txt_noise) * txt_scale
    return (jnp.clip(image_rows, -1.0, 1.0), jnp.clip(text_rows, -1.0, 1.0))


def draw_lang_order(key, part):
    return lang_maps(key)[0]


def draw_position(key, part):
    return lang_maps(key)[1]


def draw_images(key, part):
    return embed_parts(key)[0].astype(jnp.bfloat16)


def draw_texts(key, part):
    total = N_GROUP * N_DEV * ROWS
    span = N_DEV * ROWS
    ordering = lang_maps(key)[0]
    text_rows = embed_parts(key)[1]
    starts = jnp.arange(total, dtype=jnp.int32) // span * span
    return text_rows[starts + ordering].astype(jnp.bfloat16)


def setup_inputs(seed: int = 0) -> dict:
    key_of = jax.random.split(jax.random.key(seed), 7)
    images = draw_images(jax.random.fold_in(key_of[6], 71), 0)
    texts = draw_texts(jax.random.fold_in(key_of[6], 71), 0)
    lang_order = draw_lang_order(jax.random.fold_in(key_of[6], 71), 0)
    position = draw_position(jax.random.fold_in(key_of[6], 71), 0)
    logit_scale = jnp.clip(jnp.exp(jax.random.uniform(key_of[4], (1,), jnp.float32, math.log(8.0), math.log(24.0))), 8.0, 24.0)
    logit_bias = jnp.clip(jax.random.uniform(key_of[5], (1,), jnp.float32, -4.0, -1.0), -4.0, -1.0)
    return dict(images=images, texts=texts, lang_order=lang_order, position=position, logit_scale=logit_scale, logit_bias=logit_bias)


EPSILON = 1e-06

def normalize(values):
    wide = values.astype(jnp.float32)
    recip = lax.rsqrt(lax.optimization_barrier(jnp.sum(wide * wide, axis=1, keepdims=True)) + EPSILON)
    return (wide * recip, recip)

def project_back(unit, recip, grad):
    return recip * (grad - unit * lax.optimization_barrier(jnp.sum(unit * grad, axis=1, keepdims=True)))

def reference(images, texts, lang_order, position, logit_scale, logit_bias):
    span = ROWS * N_DEV
    total = span * N_GROUP
    img_unit, img_recip = normalize(images)
    txt_unit, txt_recip = normalize(texts)
    img_half = img_unit.astype(jnp.bfloat16).astype(jnp.float32)
    txt_half = txt_unit.astype(jnp.bfloat16)
    starts = jnp.arange(total, dtype=jnp.int32) // span * span
    batch_text = txt_half[starts + position.astype(jnp.int32)].astype(jnp.float32)
    scale = logit_scale[0]
    bias = logit_bias[0]
    column_ids = jnp.arange(total, dtype=jnp.int32)

    def block(carry, block_index):
        dtext, loss_sum = carry
        rows_here = lax.dynamic_slice_in_dim(img_half, (block_index * span).astype(jnp.int32), span, 0)
        logits = scale * jnp.dot(rows_here, batch_text.T, precision=lax.Precision.HIGHEST, preferred_element_type=jnp.float32) + bias
        row_ids = block_index * span + jnp.arange(span, dtype=jnp.int32)
        sign = jnp.where(row_ids[:, None] == column_ids[None, :], jnp.float32(1.0), jnp.float32(-1.0))
        loss_sum = loss_sum + jnp.sum(-jax.nn.log_sigmoid(sign * logits))
        coeff = lax.optimization_barrier((-sign * jax.nn.sigmoid(-sign * logits)).astype(jnp.bfloat16))
        coeff = coeff.astype(jnp.float32)
        dimg_block = jnp.dot(coeff, batch_text, precision=lax.Precision.HIGHEST, preferred_element_type=jnp.float32)
        dtext = dtext + jnp.dot(coeff.T, rows_here, precision=lax.Precision.HIGHEST, preferred_element_type=jnp.float32)
        return ((dtext, loss_sum), dimg_block)
    init = (jnp.zeros((total, D), jnp.float32), jnp.zeros((), jnp.float32))
    (dtext, loss_sum), dimg_blocks = lax.scan(block, init, jnp.arange(N_GROUP, dtype=jnp.int32))
    dimg = scale * dimg_blocks.reshape(total, D)
    dtext = scale * dtext
    dtext_lang = dtext[starts + lang_order.astype(jnp.int32)]
    image_grad = project_back(img_unit, img_recip, dimg)
    text_grad = project_back(txt_unit, txt_recip, dtext_lang)
    loss = (loss_sum / (jnp.float32(total) * jnp.float32(total))).reshape(1)
    return (image_grad, text_grad, loss)
```

```python
import functools

import jax
import jax.numpy as jnp
from jax import lax
from jax.experimental import pallas as pl
from jax.experimental.pallas import tpu as pltpu
from jax.sharding import PartitionSpec as P

EPSILON = 1e-06
AXES = ("group", "dev")
VMEM = pl.BlockSpec(memory_space=pltpu.VMEM)
SMEM = pl.BlockSpec(memory_space=pltpu.SMEM)


def unit_of(values):
    wide = values.astype(jnp.float32)
    recip = lax.rsqrt(jnp.sum(wide * wide, axis=1, keepdims=True) + EPSILON)
    return wide * recip, recip


def normalize_kernel(images, texts, img_half, txt_half):
    txt_half[...] = unit_of(texts[...])[0].astype(jnp.bfloat16)
    img_half[...] = unit_of(images[...])[0].astype(jnp.bfloat16)


def normalize(images, texts):
    half = jax.ShapeDtypeStruct(images.shape, jnp.bfloat16)
    return pl.pallas_call(
        normalize_kernel,
        out_shape=(half, half),
        in_specs=[VMEM] * 2,
        out_specs=(VMEM, VMEM),
        name="normalize",
    )(images, texts)


def project_kernel(count, scale, values, *refs):
    parts, out = refs[:count], refs[count]
    unit, recip = unit_of(values[...])
    total = parts[0][...]
    for part in parts[1:]:
        total = total + part[...]
    grad = scale[0] * total
    out[...] = recip * (grad - unit * jnp.sum(unit * grad, axis=1, keepdims=True))


def project(values, scale, parts, name):
    return pl.pallas_call(
        functools.partial(project_kernel, len(parts)),
        out_shape=jax.ShapeDtypeStruct(values.shape, jnp.float32),
        in_specs=[SMEM] + [VMEM] * (1 + len(parts)),
        out_specs=VMEM,
        name=name,
    )(scale, values, *parts)


def terms_kernel(own_count, block_count, pairs, first, with_loss, scale, bias, bases, *refs):
    refs = list(refs)
    own = [refs.pop(0) for _ in range(own_count)]
    blocks = [refs.pop(0) for _ in range(block_count)]
    targets = [refs.pop(0) for _ in range(own_count)]
    carried = [] if first else [refs.pop(0) for _ in range(own_count + with_loss)]
    sums = [refs.pop(0) for _ in range(own_count)]
    losses = refs.pop(0) if with_loss else None
    rows = own[0].shape[0]
    own_all = jnp.concatenate([ref[...] for ref in own], axis=0)
    if first:
        totals = None
        loss = jnp.zeros((8, 128), jnp.float32)
    else:
        totals = jnp.concatenate([ref[...] for ref in carried[:own_count]], axis=0)
        loss = carried[own_count][...] if with_loss else None
    for start in range(0, block_count, 2):
        some = range(start, min(start + 2, block_count))
        block_all = jnp.concatenate([blocks[b][...] for b in some], axis=0)
        logits = scale[0] * lax.dot_general(
            own_all, block_all, (((1,), (1,)), ((), ())), preferred_element_type=jnp.float32
        ) + bias[0]
        hits = {}
        pieces = []
        for a in range(own_count):
            strip = []
            for n, b in enumerate(some):
                piece = logits[a * rows : (a + 1) * rows, n * rows : (n + 1) * rows]
                if (a, b) in pairs:
                    ids = bases[b] + lax.broadcasted_iota(jnp.int32, (rows, rows), 1)
                    hits[a, b] = targets[a][...] == ids
                    piece = jnp.where(hits[a, b], -piece, piece)
                strip.append(piece)
            pieces.append(jnp.concatenate(strip, axis=1) if len(strip) > 1 else strip[0])
        logits = jnp.concatenate(pieces, axis=0) if own_count > 1 else pieces[0]
        small = jnp.exp(-jnp.abs(logits))
        inverse = 1.0 / (1.0 + small)
        weight = jnp.where(logits >= 0, inverse, small * inverse)
        if with_loss:
            part = jnp.maximum(logits, 0.0) + jnp.log1p(small)
            lanes = part.shape[1]
            part = jnp.sum(part.reshape(part.shape[0] // 8, 8, lanes), axis=0)
            for lane in range(0, lanes, 128):
                loss = loss + part[:, lane : lane + 128]
        pieces = []
        for a in range(own_count):
            strip = []
            for n, b in enumerate(some):
                piece = weight[a * rows : (a + 1) * rows, n * rows : (n + 1) * rows]
                if (a, b) in pairs:
                    piece = jnp.where(hits[a, b], -piece, piece)
                strip.append(piece)
            pieces.append(jnp.concatenate(strip, axis=1) if len(strip) > 1 else strip[0])
        weight = jnp.concatenate(pieces, axis=0) if own_count > 1 else pieces[0]
        term = jnp.dot(
            weight.astype(jnp.bfloat16), block_all, preferred_element_type=jnp.float32
        )
        totals = term if totals is None else totals + term
    for a in range(own_count):
        sums[a][...] = totals[a * rows : (a + 1) * rows]
    if with_loss:
        losses[...] = loss


def terms(own, blocks, targets, pairs, bases, scale, bias, carried, with_loss, name):
    rows, width = own[0].shape
    first = carried is None
    kernel = functools.partial(
        terms_kernel, len(own), len(blocks), frozenset(pairs), first, with_loss
    )
    shapes = [jax.ShapeDtypeStruct((rows, width), jnp.float32)] * len(own)
    if with_loss:
        shapes = shapes + [jax.ShapeDtypeStruct((8, 128), jnp.float32)]
    operands = [scale, bias, bases, *own, *blocks, *targets]
    base = len(operands)
    aliases = {}
    if not first:
        operands += carried
        aliases = {base + n: n for n in range(len(carried))}
    size = len(own) * len(blocks) * rows * rows
    return pl.pallas_call(
        kernel,
        out_shape=shapes,
        in_specs=[SMEM] * 3 + [VMEM] * (len(operands) - 3),
        out_specs=[VMEM] * len(shapes),
        input_output_aliases=aliases,
        cost_estimate=pl.CostEstimate(
            flops=4 * size * width,
            transcendentals=3 * size,
            bytes_accessed=(2 * len(blocks) + 10 * len(own)) * rows * width,
        ),
        name=name,
    )(*operands)


def factor(count):
    best = 1
    while (best + 1) ** 2 <= count:
        best += 1
    while count % best:
        best -= 1
    return count // best, best


def per_device(images, texts, lang_order, position, logit_scale, logit_bias):
    rows, width = images.shape
    dev_count = lax.axis_size("dev")
    group_count = lax.axis_size("group")
    cores = 2 if group_count % 2 == 0 else 1
    wide = group_count // cores
    slow, fast = factor(dev_count)
    sizes = (wide, cores, slow, fast)

    def shift(array, dim, by):
        pairs = []
        for index in range(group_count * dev_count):
            place, rest = [], index
            for size in reversed(sizes):
                place.insert(0, rest % size)
                rest //= size
            place[dim] = (place[dim] + by) % sizes[dim]
            target = 0
            for size, at in zip(sizes, place):
                target = target * size + at
            pairs.append((index, target))
        return lax.ppermute(array, AXES, pairs)

    dev_index = lax.axis_index("dev")
    slow_index, fast_index = dev_index // fast, dev_index % fast

    def base_of(slow_step, fast_step):
        at = ((slow_index - slow_step) % slow) * fast + (fast_index - fast_step) % fast
        return (at * rows).astype(jnp.int32)

    img_half, txt_half = normalize(images, texts)

    txt_line, img_line = [txt_half], [img_half]
    for _ in range(slow - 1):
        txt_line.append(shift(txt_line[-1], 2, 1))
        img_line.append(shift(img_line[-1], 2, 1))

    def spread(block, dim):
        blocks = [block]
        for _ in range(sizes[dim] - 1):
            blocks.append(shift(blocks[-1], dim, 1))
        return blocks

    def other_cores(block):
        return [shift(block, 1, by) for by in range(1, cores)]

    txt_sets = [spread(block, 3) for block in txt_line]
    img_sets = [spread(block, 0) for block in img_line]
    orders = spread(lang_order, 3)
    img_own, txt_own = img_sets[0], txt_sets[0]
    places = position.reshape(rows, 1)
    img_targets = [places] * wide
    txt_targets = [order.reshape(rows, 1) for order in orders]

    img_sums = txt_sums = None
    for step in range(slow):
        last = step == slow - 1
        for part in [(0, 1), (1, fast)] if last else [(0, fast)]:
            blocks, bases, pairs = [], [], []
            for at in range(*part):
                pairs.append((0, len(blocks)))
                blocks.append(txt_sets[step][at])
                bases.append(base_of(step, at))
                for other in other_cores(txt_sets[step][at]):
                    blocks.append(other)
                    bases.append(jnp.int32(0))
            img_sums = terms(
                img_own, blocks, img_targets, pairs, jnp.stack(bases), logit_scale, logit_bias,
                img_sums, True, "image_terms",
            )
        for part in [(0, 1), (1, wide)] if last else [(0, wide)]:
            blocks, bases, pairs = [], [], []
            for at in range(*part):
                if at == 0:
                    pairs += [(a, len(blocks)) for a in range(fast)]
                blocks.append(img_sets[step][at])
                bases.append(base_of(step, 0))
                for other in other_cores(img_sets[step][at]):
                    blocks.append(other)
                    bases.append(jnp.int32(0))
            txt_sums = terms(
                txt_own, blocks, txt_targets, pairs, jnp.stack(bases), logit_scale, logit_bias,
                txt_sums, False, "text_terms",
            )

    loss = img_sums[wide]
    for dim, size in enumerate(sizes):
        if size & (size - 1) == 0:
            by = 1
            while by < size:
                loss = loss + shift(loss, dim, by)
                by *= 2
        else:
            loss = sum((shift(loss, dim, by) for by in range(1, size)), loss)
    total = jnp.float32(rows * dev_count * group_count)
    loss = (jnp.sum(loss) / (total * total)).reshape(1)
    img_parts = [img_sums[0]] + [shift(img_sums[a], 0, -a) for a in range(1, wide)]
    txt_parts = [txt_sums[0]] + [shift(txt_sums[a], 3, -a) for a in range(1, fast)]
    image_grad = project(images, logit_scale, img_parts, "image_project")
    text_grad = project(texts, logit_scale, txt_parts, "text_project")
    return (image_grad, text_grad, loss)


def solution(mesh):
    return jax.shard_map(
        per_device,
        mesh=mesh,
        in_specs=(
            P(AXES, None),
            P(AXES, None),
            P(AXES),
            P(AXES),
            P(),
            P(),
        ),
        out_specs=(P(AXES, None), P(AXES, None), P()),
        check_vma=False,
    )
```

```python
import functools

import jax
import jax.numpy as jnp
from jax import lax
from jax.experimental import pallas as pl
from jax.experimental.pallas import tpu as pltpu
from jax.sharding import PartitionSpec as P

EPSILON = 1e-06
AXES = ("group", "dev")
VMEM = pl.BlockSpec(memory_space=pltpu.VMEM)
SMEM = pl.BlockSpec(memory_space=pltpu.SMEM)
PARAMS = pltpu.CompilerParams(vmem_limit_bytes=24 << 20)


def unit_of(values):
    wide = values.astype(jnp.float32)
    recip = lax.rsqrt(jnp.sum(wide * wide, axis=1, keepdims=True) + EPSILON)
    return wide * recip, recip


def normalize_kernel(images, texts, img_half, txt_half):
    txt_half[...] = unit_of(texts[...])[0].astype(jnp.bfloat16)
    img_half[...] = unit_of(images[...])[0].astype(jnp.bfloat16)


def normalize(images, texts):
    half = jax.ShapeDtypeStruct(images.shape, jnp.bfloat16)
    return pl.pallas_call(
        normalize_kernel,
        out_shape=(half, half),
        in_specs=[VMEM] * 2,
        out_specs=(VMEM, VMEM),
        compiler_params=PARAMS,
        name="normalize",
    )(images, texts)


def project_kernel(count, scale, values, *refs):
    parts, out = refs[:count], refs[count]
    unit, recip = unit_of(values[...])
    total = parts[0][...]
    for part in parts[1:]:
        total = total + part[...]
    grad = scale[0] * total
    out[...] = recip * (grad - unit * jnp.sum(unit * grad, axis=1, keepdims=True))


def project(values, scale, parts):
    return pl.pallas_call(
        functools.partial(project_kernel, len(parts)),
        out_shape=jax.ShapeDtypeStruct(values.shape, jnp.float32),
        in_specs=[SMEM] + [VMEM] * (1 + len(parts)),
        out_specs=VMEM,
        compiler_params=PARAMS,
    )(scale, values, *parts)


def terms_kernel(own_count, block_count, places, pairs, first, with_loss, scale, bias, bases, *refs):
    refs = list(refs)
    own = [refs.pop(0) for _ in range(own_count)]
    blocks = [refs.pop(0) for _ in range(block_count)]
    targets = [refs.pop(0) for _ in range(own_count)]
    carried = [] if first else [refs.pop(0) for _ in range(own_count + with_loss)]
    sums = [refs.pop(0) for _ in range(own_count)]
    losses = refs.pop(0) if with_loss else None
    rows = own[0].shape[0]
    columns = [
        jnp.transpose(jnp.broadcast_to(target[...], (rows, rows))) for target in targets
    ]
    own_all = jnp.concatenate([ref[...] for ref in own], axis=0)
    if first:
        totals = None
        loss = jnp.zeros((8, 128), jnp.float32)
    else:
        totals = jnp.concatenate([ref[...] for ref in carried[:own_count]], axis=0)
        loss = carried[own_count][...] if with_loss else None
    for start in range(0, block_count, 2):
        some = range(start, min(start + 2, block_count))
        block_all = jnp.concatenate([blocks[b][...] for b in some], axis=0)
        logits = scale[0] * lax.dot_general(
            own_all, block_all, (((1,), (1,)), ((), ())), preferred_element_type=jnp.float32
        ) + bias[0]
        hits = {}
        pieces = []
        for a in range(own_count):
            strip = []
            for n, b in enumerate(some):
                piece = logits[a * rows : (a + 1) * rows, n * rows : (n + 1) * rows]
                if (a, b) in pairs:
                    ids = bases[places[b]] + lax.broadcasted_iota(jnp.int32, (rows, rows), 1)
                    hits[a, b] = columns[a] == ids
                    piece = jnp.where(hits[a, b], -piece, piece)
                strip.append(piece)
            pieces.append(jnp.concatenate(strip, axis=1) if len(strip) > 1 else strip[0])
        logits = jnp.concatenate(pieces, axis=0) if own_count > 1 else pieces[0]
        small = jnp.exp(-jnp.abs(logits))
        inverse = 1.0 / (1.0 + small)
        weight = jnp.where(logits >= 0, inverse, small * inverse)
        if with_loss:
            part = jnp.maximum(logits, 0.0) + jnp.log1p(small)
            lanes = part.shape[1]
            part = jnp.sum(part.reshape(part.shape[0] // 8, 8, lanes), axis=0)
            for lane in range(0, lanes, 128):
                loss = loss + part[:, lane : lane + 128]
        pieces = []
        for a in range(own_count):
            strip = []
            for n, b in enumerate(some):
                piece = weight[a * rows : (a + 1) * rows, n * rows : (n + 1) * rows]
                if (a, b) in pairs:
                    piece = jnp.where(hits[a, b], -piece, piece)
                strip.append(piece)
            pieces.append(jnp.concatenate(strip, axis=1) if len(strip) > 1 else strip[0])
        weight = jnp.concatenate(pieces, axis=0) if own_count > 1 else pieces[0]
        term = jnp.dot(
            weight.astype(jnp.bfloat16), block_all, preferred_element_type=jnp.float32
        )
        totals = term if totals is None else totals + term
    for a in range(own_count):
        sums[a][...] = totals[a * rows : (a + 1) * rows]
    if with_loss:
        losses[...] = loss


def terms(own, blocks, places, targets, pairs, bases, scale, bias, carried, with_loss):
    rows, width = own[0].shape
    first = carried is None
    kernel = functools.partial(
        terms_kernel, len(own), len(blocks), tuple(places), frozenset(pairs), first, with_loss
    )
    shapes = [jax.ShapeDtypeStruct((rows, width), jnp.float32)] * len(own)
    if with_loss:
        shapes = shapes + [jax.ShapeDtypeStruct((8, 128), jnp.float32)]
    operands = [scale, bias, bases, *own, *blocks, *targets]
    base = len(operands)
    aliases = {}
    if not first:
        operands += carried
        aliases = {base + n: n for n in range(len(carried))}
    size = len(own) * len(blocks) * rows * rows
    return pl.pallas_call(
        kernel,
        out_shape=shapes,
        in_specs=[SMEM] * 3 + [VMEM] * (len(operands) - 3),
        out_specs=[VMEM] * len(shapes),
        input_output_aliases=aliases,
        cost_estimate=pl.CostEstimate(
            flops=4 * size * width,
            transcendentals=3 * size,
            bytes_accessed=(2 * len(blocks) + 10 * len(own)) * rows * width,
        ),
        compiler_params=PARAMS,
    )(*operands)


def factor(count):
    best = 1
    while (best + 1) ** 2 <= count:
        best += 1
    while count % best:
        best -= 1
    return count // best, best


def per_device(images, texts, lang_order, position, logit_scale, logit_bias):
    rows, _ = images.shape
    dev_count = lax.axis_size("dev")
    group_count = lax.axis_size("group")
    cores = 2 if group_count % 2 == 0 else 1
    wide = group_count // cores
    slow, fast = factor(dev_count)
    sizes = (wide, cores, slow, fast)

    def shift(array, dim, by):
        pairs = []
        for index in range(group_count * dev_count):
            place, rest = [], index
            for size in reversed(sizes):
                place.insert(0, rest % size)
                rest //= size
            place[dim] = (place[dim] + by) % sizes[dim]
            target = 0
            for size, at in zip(sizes, place):
                target = target * size + at
            pairs.append((index, target))
        return lax.ppermute(array, AXES, pairs)

    dev_index = lax.axis_index("dev")
    slow_index, fast_index = dev_index // fast, dev_index % fast
    offsets = jnp.arange(slow * fast, dtype=jnp.int32)
    bases = rows * (
        (slow_index - offsets // fast) % slow * fast + (fast_index - offsets % fast) % fast
    )
    bases = bases.astype(jnp.int32)

    img_half, txt_half = normalize(images, texts)

    def spread(block, dim):
        blocks = [block]
        for _ in range(sizes[dim] - 1):
            blocks.append(shift(blocks[-1], dim, 1))
        return blocks

    def with_cores(blocks):
        out = []
        for block in blocks:
            out.append([block] + [shift(block, 1, by) for by in range(1, cores)])
        return out

    orders = spread(lang_order.reshape(1, rows), 3)
    img_targets = [position.reshape(1, rows)] * wide
    txt_targets = orders

    txt_line, img_line, txt_sets, img_sets = [txt_half], [img_half], [], []
    for step in range(slow):
        if step:
            txt_line.append(shift(txt_line[-1], 2, 1))
            img_line.append(shift(img_line[-1], 2, 1))
        txt_sets.append(with_cores(spread(txt_line[-1], 3)))
        img_sets.append(with_cores(spread(img_line[-1], 0)))
    img_own = [cores_of[0] for cores_of in img_sets[0]]
    txt_own = [cores_of[0] for cores_of in txt_sets[0]]

    def gradient(own, targets, sets, sums, step, part, with_loss):
        blocks, places, pairs = [], [], []
        for at in range(*part):
            if with_loss:
                pairs.append((0, len(blocks)))
            elif at == 0:
                pairs += [(a, len(blocks)) for a in range(len(own))]
            for block in sets[step][at]:
                blocks.append(block)
                places.append(step * fast + (at if with_loss else 0))
        return terms(
            own, blocks, places, targets, pairs, bases, logit_scale, logit_bias, sums,
            with_loss,
        )

    img_sums = txt_sums = None
    for step in range(slow):
        tail = step == slow - 1
        for part in [(0, 1), (1, fast)] if tail and fast > 1 else [(0, fast)]:
            img_sums = gradient(img_own, img_targets, txt_sets, img_sums, step, part, True)
        for part in [(0, 1), (1, wide)] if tail and wide > 1 else [(0, wide)]:
            txt_sums = gradient(txt_own, txt_targets, img_sets, txt_sums, step, part, False)

    loss = img_sums[wide]
    for dim in (0, 3, 1, 2):
        size = sizes[dim]
        if size & (size - 1) == 0:
            by = 1
            while by < size:
                loss = loss + shift(loss, dim, by)
                by = 2 * by
        else:
            loss = sum((shift(loss, dim, by) for by in range(1, size)), loss)
    total = jnp.float32(rows * dev_count * group_count)
    loss = (jnp.sum(loss) / (total * total)).reshape(1)
    img_parts = [img_sums[0]] + [shift(img_sums[a], 0, -a) for a in range(1, wide)]
    txt_parts = [txt_sums[0]] + [shift(txt_sums[a], 3, -a) for a in range(1, fast)]
    image_grad = project(images, logit_scale, img_parts)
    text_grad = project(texts, logit_scale, txt_parts)
    return (image_grad, text_grad, loss)


def solution(mesh):
    return jax.shard_map(
        per_device,
        mesh=mesh,
        in_specs=(
            P(AXES, None),
            P(AXES, None),
            P(AXES),
            P(AXES),
            P(),
            P(),
        ),
        out_specs=(P(AXES, None), P(AXES, None), P()),
        check_vma=False,
    )
```

```python
import functools

import jax
import jax.numpy as jnp
from jax import lax
from jax.experimental import pallas as pl
from jax.experimental.pallas import tpu as pltpu
from jax.sharding import PartitionSpec as P

EPSILON = 1e-06
AXES = ("group", "dev")
VMEM = pl.BlockSpec(memory_space=pltpu.VMEM)
PARAMS = pltpu.CompilerParams(vmem_limit_bytes=16 << 20)


def unit_of(values):
    wide = values.astype(jnp.float32)
    recip = lax.rsqrt(jnp.sum(wide * wide, axis=1, keepdims=True) + EPSILON)
    return wide * recip, recip


def normalize_kernel(values, half):
    half[...] = unit_of(values[...])[0].astype(jnp.bfloat16)


def normalize(values):
    return pl.pallas_call(
        normalize_kernel,
        out_shape=jax.ShapeDtypeStruct(values.shape, jnp.bfloat16),
        in_specs=[VMEM],
        out_specs=VMEM,
        compiler_params=PARAMS,
    )(values)


def project_kernel(count, settings, values, *refs):
    parts, out = refs[:count], refs[count]
    unit, recip = unit_of(values[...])
    total = parts[0][...]
    for part in parts[1:]:
        total = total + part[...]
    grad = settings[0:1, 0:1] * total
    out[...] = recip * (grad - unit * jnp.sum(unit * grad, axis=1, keepdims=True))


def project(values, settings, parts):
    return pl.pallas_call(
        functools.partial(project_kernel, len(parts)),
        out_shape=jax.ShapeDtypeStruct(values.shape, jnp.float32),
        in_specs=[VMEM] * (2 + len(parts)),
        out_specs=VMEM,
        compiler_params=PARAMS,
    )(settings, values, *parts)


def terms_kernel(
    own_count, block_count, places, pairs, first, with_loss, settings, ids, *refs
):
    refs = list(refs)
    own = [refs.pop(0) for _ in range(own_count)]
    blocks = [refs.pop(0) for _ in range(block_count)]
    targets = [refs.pop(0) for _ in range(own_count)]
    carried = [] if first else [refs.pop(0) for _ in range(own_count + with_loss)]
    sums = [refs.pop(0) for _ in range(own_count)]
    losses = refs.pop(0) if with_loss else None
    own_rows, block_rows = own[0].shape[0], blocks[0].shape[0]
    columns = {}
    for a, _ in sorted(pairs):
        if a not in columns:
            spread = jnp.broadcast_to(targets[a][...], (own_rows, own_rows))
            columns[a] = jnp.transpose(spread)[:, :1]
    if with_loss:
        loss = jnp.zeros((8, 128), jnp.float32) if first else carried[own_count][...]

    def weigh(a, b, dot):
        nonlocal loss
        logits = settings[0:1, :block_rows] * dot + settings[4:5, :block_rows]
        hit = None
        if (a, b) in pairs:
            at, offset = places[b]
            hit = columns[a] == ids[at : at + 1, offset : offset + block_rows]
            logits = jnp.where(hit, -logits, logits)
        small = jnp.exp(-jnp.abs(logits))
        inverse = 1.0 / (1.0 + small)
        weight = jnp.where(logits >= 0, inverse, small * inverse)
        if with_loss:
            part = jnp.maximum(logits, 0.0) + jnp.log1p(small)
            part = jnp.sum(part.reshape(own_rows // 8, 8, block_rows), axis=0)
            for lane in range(0, block_rows, 128):
                loss = loss + part[:, lane : lane + 128]
        if hit is not None:
            weight = jnp.where(hit, -weight, weight)
        return weight.astype(jnp.bfloat16)

    own_all = jnp.concatenate([ref[...] for ref in own], axis=0) if own_count > 1 else own[0][...]
    weights = [[] for _ in own]
    chosen = []
    group = max(1, 256 // block_rows)
    for start in range(0, block_count, group):
        some = range(start, min(start + group, block_count))
        block_all = jnp.concatenate([blocks[b][...] for b in some], axis=0)
        chosen.append(block_all)
        dots = lax.dot_general(
            own_all, block_all, (((1,), (1,)), ((), ())), preferred_element_type=jnp.float32
        )
        for a in range(own_count):
            for n, b in enumerate(some):
                dot = dots[
                    a * own_rows : (a + 1) * own_rows, n * block_rows : (n + 1) * block_rows
                ]
                weights[a].append(weigh(a, b, dot))
    weight_all = jnp.concatenate([jnp.concatenate(row, axis=1) for row in weights], axis=0)
    block_all = jnp.concatenate(chosen, axis=0)
    term = jnp.dot(weight_all, block_all, preferred_element_type=jnp.float32)
    for a in range(own_count):
        part = term[a * own_rows : (a + 1) * own_rows]
        sums[a][...] = part if first else carried[a][...] + part
    if with_loss:
        losses[...] = loss


def terms(own, blocks, places, targets, pairs, ids, settings, carried, with_loss):
    rows, width = own[0].shape
    first = carried is None
    kernel = functools.partial(
        terms_kernel, len(own), len(blocks), tuple(places), frozenset(pairs), first, with_loss
    )
    shapes = [jax.ShapeDtypeStruct((rows, width), jnp.float32)] * len(own)
    if with_loss:
        shapes = shapes + [jax.ShapeDtypeStruct((8, 128), jnp.float32)]
    operands = [settings, ids, *own, *blocks, *targets]
    base = len(operands)
    aliases = {}
    if not first:
        operands += carried
        aliases = {base + n: n for n in range(len(carried))}
    size = len(own) * len(blocks) * rows * blocks[0].shape[0]
    return pl.pallas_call(
        kernel,
        out_shape=shapes,
        in_specs=[VMEM] * len(operands),
        out_specs=[VMEM] * len(shapes),
        input_output_aliases=aliases,
        cost_estimate=pl.CostEstimate(
            flops=4 * size * width,
            transcendentals=3 * size,
            bytes_accessed=(2 * len(blocks) + 10 * len(own)) * rows * width,
        ),
        compiler_params=PARAMS,
    )(*operands)


def factor(count):
    best = 1
    while (best + 1) ** 2 <= count:
        best += 1
    while count % best:
        best -= 1
    return count // best, best


def per_device(images, texts, lang_order, position, logit_scale, logit_bias):
    rows, _ = images.shape
    dev_count = lax.axis_size("dev")
    group_count = lax.axis_size("group")
    cores = 2 if group_count % 2 == 0 else 1
    wide = group_count // cores
    slow, fast = factor(dev_count)
    sizes = (wide, cores, slow, fast)

    def permuted(array, dim, move):
        pairs = []
        for index in range(group_count * dev_count):
            place, rest = [], index
            for size in reversed(sizes):
                place.insert(0, rest % size)
                rest //= size
            place[dim] = move(place[dim])
            target = 0
            for size, at in zip(sizes, place):
                target = target * size + at
            pairs.append((index, target))
        return lax.ppermute(array, AXES, pairs)

    def shift(array, dim, by):
        return permuted(array, dim, lambda at: (at + by) % sizes[dim])

    def exchange(array, dim, by):
        return permuted(array, dim, lambda at: at ^ by)

    dev_index = lax.axis_index("dev")
    slow_index, fast_index = dev_index // fast, dev_index % fast
    offsets = jnp.arange(slow * fast, dtype=jnp.int32)
    bases = (slow_index - offsets // fast) % slow * fast + (fast_index - offsets % fast) % fast
    ids = (rows * bases[:, None] + jnp.arange(rows, dtype=jnp.int32)[None, :]).astype(jnp.int32)
    settings = jnp.concatenate(
        [
            jnp.broadcast_to(logit_scale[:, None], (4, rows)),
            jnp.broadcast_to(logit_bias[:, None], (4, rows)),
        ],
        axis=0,
    )

    txt_half = normalize(texts)
    img_half = normalize(images)

    def spread(block, dim):
        blocks = [block]
        for _ in range(sizes[dim] - 1):
            blocks.append(shift(blocks[-1], dim, 1))
        return blocks

    def with_cores(blocks):
        out = []
        for block in blocks:
            out.append([block] + [shift(block, 1, by) for by in range(1, cores)])
        return out

    img_targets = [position.reshape(1, rows)] * wide
    txt_targets = spread(lang_order.reshape(1, rows), 3)

    def txt_blocks(block):
        return with_cores(spread(block, 3))

    def img_blocks(block):
        return with_cores(spread(block, 0))

    end = slow - 1
    middle = rows // 2
    txt_line, img_line, txt_sets, img_sets = [txt_half], [img_half], [], []
    for step in range(slow):
        if step:
            txt_line.append(shift(txt_line[-1], 2, 1))
        txt_sets.append(txt_blocks(txt_line[-1]))
        if step < end:
            if step:
                img_line.append(shift(img_line[-1], 2, 1))
            img_sets.append(img_blocks(img_line[-1]))
    first = shift(img_line[-1][:middle], 2, 1)
    second = shift(img_line[-1][middle:], 2, 1)
    first_set, second_set = img_blocks(first), img_blocks(second)
    img_own = [cores_of[0] for cores_of in img_sets[0]]
    txt_own = [cores_of[0] for cores_of in txt_sets[0]]

    def image_terms(sums, parts):
        blocks, places, pairs = [], [], []
        for step, at in parts:
            pairs.append((0, len(blocks)))
            for block in txt_sets[step][at]:
                blocks.append(block)
                places.append((step * fast + at, 0))
        return terms(img_own, blocks, places, img_targets, pairs, ids, settings, sums, True)

    def text_terms(sums, parts):
        blocks, places, pairs = [], [], []
        for cores_of, step, at, offset in parts:
            if at == 0:
                pairs += [(a, len(blocks)) for a in range(fast)]
            for block in cores_of:
                blocks.append(block)
                places.append((step * fast, offset))
        return terms(txt_own, blocks, places, txt_targets, pairs, ids, settings, sums, False)

    img_sums = txt_sums = None
    for step in range(end):
        parts = [(step, at) for at in range(fast)]
        if step == end - 1:
            parts.append((end, 0))
        img_sums = image_terms(img_sums, parts)
        parts = [(img_sets[step][at], step, at, 0) for at in range(wide)]
        txt_sums = text_terms(txt_sums, parts)
    halves = [(first_set, 0), (second_set, middle)]
    txt_sums = text_terms(txt_sums, [(half[0], end, 0, offset) for half, offset in halves])
    if fast > 1:
        img_sums = image_terms(img_sums, [(end, at) for at in range(1, fast)])
    if wide > 1:
        parts = [(half[at], end, at, offset) for at in range(1, wide) for half, offset in halves]
        txt_sums = text_terms(txt_sums, parts)

    loss = img_sums[wide]
    for dim in (0, 3, 1, 2):
        size = sizes[dim]
        if size & (size - 1) == 0:
            by = 1
            while by < size:
                loss = loss + exchange(loss, dim, by)
                by = 2 * by
        else:
            loss = sum((shift(loss, dim, by) for by in range(1, size)), loss)
    total = jnp.float32(rows * dev_count * group_count)
    loss = (jnp.sum(loss) / (total * total)).reshape(1)
    img_parts = [img_sums[0]] + [shift(img_sums[a], 0, -a) for a in range(1, wide)]
    txt_parts = [txt_sums[0]] + [shift(txt_sums[a], 3, -a) for a in range(1, fast)]
    image_grad = project(images, settings, img_parts)
    text_grad = project(texts, settings, txt_parts)
    return (image_grad, text_grad, loss)


def solution(mesh):
    return jax.shard_map(
        per_device,
        mesh=mesh,
        in_specs=(
            P(AXES, None),
            P(AXES, None),
            P(AXES),
            P(AXES),
            P(),
            P(),
        ),
        out_specs=(P(AXES, None), P(AXES, None), P()),
        check_vma=False,
    )
```

```python
import functools

import jax
import jax.numpy as jnp
from jax import lax
from jax.experimental import pallas as pl
from jax.experimental.pallas import tpu as pltpu
from jax.sharding import PartitionSpec as P

EPSILON = 1e-06
AXES = ("group", "dev")
VMEM = pl.BlockSpec(memory_space=pltpu.VMEM)
PARAMS = pltpu.CompilerParams(vmem_limit_bytes=16 << 20)


def unit_of(values):
    wide = values.astype(jnp.float32)
    recip = lax.rsqrt(jnp.sum(wide * wide, axis=1, keepdims=True) + EPSILON)
    return wide * recip, recip


def normalize_kernel(values, half):
    half[...] = unit_of(values[...])[0].astype(jnp.bfloat16)


def normalize(values):
    return pl.pallas_call(
        normalize_kernel,
        out_shape=jax.ShapeDtypeStruct(values.shape, jnp.bfloat16),
        in_specs=[VMEM],
        out_specs=VMEM,
        compiler_params=PARAMS,
    )(values)


def project_kernel(count, settings, values, *refs):
    parts, out = refs[:count], refs[count]
    unit, recip = unit_of(values[...])
    total = parts[0][...]
    for part in parts[1:]:
        total = total + part[...]
    grad = settings[0:1, 0:1] * total
    out[...] = recip * (grad - unit * jnp.sum(unit * grad, axis=1, keepdims=True))


def project(values, settings, parts):
    return pl.pallas_call(
        functools.partial(project_kernel, len(parts)),
        out_shape=jax.ShapeDtypeStruct(values.shape, jnp.float32),
        in_specs=[VMEM] * (2 + len(parts)),
        out_specs=VMEM,
        compiler_params=PARAMS,
    )(settings, values, *parts)


def terms_kernel(
    own_count, block_count, places, pairs, first, loss_own, loss_first, settings, ids, *refs
):
    refs = list(refs)
    own = [refs.pop(0) for _ in range(own_count)]
    blocks = [refs.pop(0) for _ in range(block_count)]
    targets = [refs.pop(0) for _ in range(own_count)]
    carried = [] if first else [refs.pop(0) for _ in range(own_count)]
    loss_in = refs.pop(0) if loss_own and not loss_first else None
    sums = [refs.pop(0) for _ in range(own_count)]
    losses = refs.pop(0) if loss_own else None
    own_rows, block_rows = own[0].shape[0], blocks[0].shape[0]
    columns = {}
    for a, _ in sorted(pairs):
        if a not in columns:
            spread = jnp.broadcast_to(targets[a][...], (own_rows, own_rows))
            columns[a] = jnp.transpose(spread)[:, :1]
    loss = None
    if loss_own:
        loss = jnp.zeros((8, 128), jnp.float32) if loss_first else loss_in[...]

    def weigh(a, b, dot):
        nonlocal loss
        logits = settings[0:1, :block_rows] * dot + settings[4:5, :block_rows]
        hit = None
        if (a, b) in pairs:
            at, offset = places[b]
            hit = columns[a] == ids[at : at + 1, offset : offset + block_rows]
            logits = jnp.where(hit, -logits, logits)
        small = jnp.exp(-jnp.abs(logits))
        inverse = 1.0 / (1.0 + small)
        weight = jnp.where(logits >= 0, inverse, small * inverse)
        if a in loss_own:
            part = jnp.maximum(logits, 0.0) + jnp.log1p(small)
            part = jnp.sum(part.reshape(own_rows // 8, 8, block_rows), axis=0)
            for lane in range(0, block_rows, 128):
                loss = loss + part[:, lane : lane + 128]
        if hit is not None:
            weight = jnp.where(hit, -weight, weight)
        return weight.astype(jnp.bfloat16)

    own_all = jnp.concatenate([ref[...] for ref in own], axis=0) if own_count > 1 else own[0][...]
    weights = [[] for _ in own]
    chosen = []
    group = max(1, 256 // block_rows)
    for start in range(0, block_count, group):
        some = range(start, min(start + group, block_count))
        block_all = jnp.concatenate([blocks[b][...] for b in some], axis=0)
        chosen.append(block_all)
        dots = lax.dot_general(
            own_all, block_all, (((1,), (1,)), ((), ())), preferred_element_type=jnp.float32
        )
        for a in range(own_count):
            for n, b in enumerate(some):
                dot = dots[
                    a * own_rows : (a + 1) * own_rows, n * block_rows : (n + 1) * block_rows
                ]
                weights[a].append(weigh(a, b, dot))
    weight_all = jnp.concatenate([jnp.concatenate(row, axis=1) for row in weights], axis=0)
    block_all = jnp.concatenate(chosen, axis=0)
    term = jnp.dot(weight_all, block_all, preferred_element_type=jnp.float32)
    for a in range(own_count):
        part = term[a * own_rows : (a + 1) * own_rows]
        sums[a][...] = part if first else carried[a][...] + part
    if loss_own:
        losses[...] = loss


def terms(own, blocks, places, targets, pairs, ids, settings, sums, loss_own, loss):
    rows, width = own[0].shape
    kernel = functools.partial(
        terms_kernel,
        len(own),
        len(blocks),
        tuple(places),
        frozenset(pairs),
        sums is None,
        tuple(loss_own),
        loss is None,
    )
    shapes = [jax.ShapeDtypeStruct((rows, width), jnp.float32)] * len(own)
    if loss_own:
        shapes = shapes + [jax.ShapeDtypeStruct((8, 128), jnp.float32)]
    operands = [settings, ids, *own, *blocks, *targets]
    aliases = {}
    if sums is not None:
        aliases = {len(operands) + n: n for n in range(len(own))}
        operands += sums
    if loss_own and loss is not None:
        aliases[len(operands)] = len(own)
        operands.append(loss)
    size = len(own) * len(blocks) * rows * blocks[0].shape[0]
    out = pl.pallas_call(
        kernel,
        out_shape=shapes,
        in_specs=[VMEM] * len(operands),
        out_specs=[VMEM] * len(shapes),
        input_output_aliases=aliases,
        cost_estimate=pl.CostEstimate(
            flops=4 * size * width,
            transcendentals=3 * size,
            bytes_accessed=(2 * len(blocks) + 10 * len(own)) * rows * width,
        ),
        compiler_params=PARAMS,
    )(*operands)
    return out[: len(own)], out[len(own)] if loss_own else loss


def factor(count):
    best = 1
    while (best + 1) ** 2 <= count:
        best += 1
    while count % best:
        best -= 1
    return count // best, best


def per_device(images, texts, lang_order, position, logit_scale, logit_bias):
    rows, _ = images.shape
    dev_count = lax.axis_size("dev")
    group_count = lax.axis_size("group")
    cores = 2 if group_count % 2 == 0 else 1
    wide = group_count // cores
    slow, fast = factor(dev_count)
    sizes = (wide, cores, slow, fast)

    def permuted(array, dim, move):
        pairs = []
        for index in range(group_count * dev_count):
            place, rest = [], index
            for size in reversed(sizes):
                place.insert(0, rest % size)
                rest //= size
            place[dim] = move(place[dim])
            target = 0
            for size, at in zip(sizes, place):
                target = target * size + at
            pairs.append((index, target))
        return lax.ppermute(array, AXES, pairs)

    def shift(array, dim, by):
        return permuted(array, dim, lambda at: (at + by) % sizes[dim])

    def exchange(array, dim, by):
        return permuted(array, dim, lambda at: at ^ by)

    dev_index = lax.axis_index("dev")
    slow_index, fast_index = dev_index // fast, dev_index % fast
    offsets = jnp.arange(slow * fast, dtype=jnp.int32)
    bases = (slow_index - offsets // fast) % slow * fast + (fast_index - offsets % fast) % fast
    ids = (rows * bases[:, None] + jnp.arange(rows, dtype=jnp.int32)[None, :]).astype(jnp.int32)
    settings = jnp.concatenate(
        [
            jnp.broadcast_to(logit_scale[:, None], (4, rows)),
            jnp.broadcast_to(logit_bias[:, None], (4, rows)),
        ],
        axis=0,
    )

    txt_half = normalize(texts)
    img_half = normalize(images)

    def spread(block, dim):
        blocks = [block]
        for _ in range(sizes[dim] - 1):
            blocks.append(shift(blocks[-1], dim, 1))
        return blocks

    def with_cores(blocks):
        out = []
        for block in blocks:
            out.append([block] + [shift(block, 1, by) for by in range(1, cores)])
        return out

    img_targets = [position.reshape(1, rows)] * wide
    txt_targets = spread(lang_order.reshape(1, rows), 3)

    def txt_blocks(block):
        return with_cores(spread(block, 3))

    def img_blocks(block):
        return with_cores(spread(block, 0))

    end = slow - 1
    middle = rows // 2
    txt_line, img_line, txt_sets, img_sets = [txt_half], [img_half], [], []
    for step in range(slow):
        if step:
            txt_line.append(shift(txt_line[-1], 2, 1))
        txt_sets.append(txt_blocks(txt_line[-1]))
        if step < end:
            if step:
                img_line.append(shift(img_line[-1], 2, 1))
            img_sets.append(img_blocks(img_line[-1]))
    first = shift(img_line[-1][:middle], 2, 1)
    second = shift(img_line[-1][middle:], 2, 1)
    first_set, second_set = img_blocks(first), img_blocks(second)
    img_own = [cores_of[0] for cores_of in img_sets[0]]
    txt_own = [cores_of[0] for cores_of in txt_sets[0]]

    def image_terms(sums, loss, parts, counted=True):
        blocks, places, pairs = [], [], []
        for step, at in parts:
            pairs.append((0, len(blocks)))
            for block in txt_sets[step][at]:
                blocks.append(block)
                places.append((step * fast + at, 0))
        loss_own = range(wide) if counted else ()
        return terms(
            img_own, blocks, places, img_targets, pairs, ids, settings, sums, loss_own, loss,
        )

    def text_terms(sums, loss, parts, loss_own=()):
        blocks, places, pairs = [], [], []
        for cores_of, step, at, offset in parts:
            if at == 0:
                pairs += [(a, len(blocks)) for a in range(fast)]
            for block in cores_of:
                blocks.append(block)
                places.append((step * fast, offset))
        return terms(
            txt_own, blocks, places, txt_targets, pairs, ids, settings, sums, loss_own, loss,
        )

    img_sums = txt_sums = loss = None
    for step in range(end):
        parts = [(step, at) for at in range(fast)]
        if step == end - 1:
            parts.append((end, 0))
        img_sums, loss = image_terms(img_sums, loss, parts)
        parts = [(img_sets[step][at], step, at, 0) for at in range(wide)]
        counted = range(1, fast) if step == 1 else ()
        txt_sums, loss = text_terms(txt_sums, loss, parts, counted)
    halves = [(first_set, 0), (second_set, middle)]
    txt_sums, loss = text_terms(
        txt_sums, loss, [(half[0], end, 0, offset) for half, offset in halves],
        range(1, fast) if end == 1 else (),
    )
    if fast > 1:
        parts = [(end, at) for at in range(1, fast)]
        img_sums, loss = image_terms(img_sums, loss, parts, False)
    if wide > 1:
        parts = [(half[at], end, at, offset) for at in range(1, wide) for half, offset in halves]
        txt_sums, loss = text_terms(txt_sums, loss, parts, range(1, fast) if end == 1 else ())

    for dim in (0, 3, 1, 2):
        size = sizes[dim]
        if size & (size - 1) == 0:
            by = 1
            while by < size:
                loss = loss + exchange(loss, dim, by)
                by = 2 * by
        else:
            loss = sum((shift(loss, dim, by) for by in range(1, size)), loss)
    total = jnp.float32(rows * dev_count * group_count)
    loss = (jnp.sum(loss) / (total * total)).reshape(1)
    img_parts = [img_sums[0]] + [shift(img_sums[a], 0, -a) for a in range(1, wide)]
    txt_parts = [txt_sums[0]] + [shift(txt_sums[a], 3, -a) for a in range(1, fast)]
    image_grad = project(images, settings, img_parts)
    text_grad = project(texts, settings, txt_parts)
    return (image_grad, text_grad, loss)


def solution(mesh):
    return jax.shard_map(
        per_device,
        mesh=mesh,
        in_specs=(
            P(AXES, None),
            P(AXES, None),
            P(AXES),
            P(AXES),
            P(),
            P(),
        ),
        out_specs=(P(AXES, None), P(AXES, None), P()),
        check_vma=False,
    )
```

```python
import functools

import jax
import jax.numpy as jnp
from jax import lax
from jax.experimental import pallas as pl
from jax.experimental.pallas import tpu as pltpu
from jax.sharding import PartitionSpec as P

EPSILON = 1e-06
AXES = ("group", "dev")
VMEM = pl.BlockSpec(memory_space=pltpu.VMEM)
PARAMS = pltpu.CompilerParams(vmem_limit_bytes=16 << 20)


def unit_of(values):
    wide = values.astype(jnp.float32)
    recip = lax.rsqrt(jnp.sum(wide * wide, axis=1, keepdims=True) + EPSILON)
    return wide * recip, recip


def normalize_kernel(values, half):
    half[...] = unit_of(values[...])[0].astype(jnp.bfloat16)


def normalize(values):
    return pl.pallas_call(
        normalize_kernel,
        out_shape=jax.ShapeDtypeStruct(values.shape, jnp.bfloat16),
        in_specs=[VMEM],
        out_specs=VMEM,
        compiler_params=PARAMS,
    )(values)


def project_kernel(count, loss_count, factor, settings, values, *refs):
    parts, losses, out = refs[:count], refs[count : count + loss_count], refs[count + loss_count]
    unit, recip = unit_of(values[...])
    total = parts[0][...]
    for part in parts[1:]:
        total = total + part[...]
    grad = settings[0:1, 0:1] * total
    out[...] = recip * (grad - unit * jnp.sum(unit * grad, axis=1, keepdims=True))
    if loss_count:
        loss = losses[0][...]
        for part in losses[1:]:
            loss = loss + part[...]
        refs[-1][0] = factor * jnp.sum(loss)


def project(values, settings, parts, losses, factor):
    shapes = [jax.ShapeDtypeStruct(values.shape, jnp.float32)]
    specs = [VMEM]
    if losses:
        shapes.append(jax.ShapeDtypeStruct((1,), jnp.float32))
        specs.append(pl.BlockSpec(memory_space=pltpu.SMEM))
    out = pl.pallas_call(
        functools.partial(project_kernel, len(parts), len(losses), factor),
        out_shape=shapes,
        in_specs=[VMEM] * (2 + len(parts) + len(losses)),
        out_specs=specs,
        compiler_params=PARAMS,
    )(settings, values, *parts, *losses)
    return tuple(out) if losses else out[0]


def terms_kernel(
    own_count, block_count, places, pairs, first, loss_own, loss_first, settings, ids, *refs
):
    refs = list(refs)
    own = [refs.pop(0) for _ in range(own_count)]
    blocks = [refs.pop(0) for _ in range(block_count)]
    targets = [refs.pop(0) for _ in range(own_count)]
    carried = [] if first else [refs.pop(0) for _ in range(own_count)]
    loss_in = refs.pop(0) if loss_own and not loss_first else None
    sums = [refs.pop(0) for _ in range(own_count)]
    losses = refs.pop(0) if loss_own else None
    own_rows = own[0].shape[0]
    columns = {}
    for a, _ in sorted(pairs):
        if a not in columns:
            spread = jnp.broadcast_to(targets[a][...], (own_rows, own_rows))
            columns[a] = jnp.transpose(spread)[:, :1]
    loss = None
    if loss_own:
        loss = jnp.zeros((8, 128), jnp.float32) if loss_first else loss_in[...]

    def weigh(a, b, dot):
        nonlocal loss
        block_rows = dot.shape[1]
        logits = settings[0:1, :block_rows] * dot + settings[4:5, :block_rows]
        hit = None
        if (a, b) in pairs:
            at, offset = places[b]
            hit = columns[a] == ids[at : at + 1, offset : offset + block_rows]
            logits = jnp.where(hit, -logits, logits)
        small = jnp.exp(-jnp.abs(logits))
        inverse = 1.0 / (1.0 + small)
        weight = jnp.where(logits >= 0, inverse, small * inverse)
        if a in loss_own:
            part = jnp.maximum(logits, 0.0) + jnp.log1p(small)
            part = jnp.sum(part.reshape(own_rows // 8, 8, block_rows), axis=0)
            for lane in range(0, block_rows, 128):
                loss = loss + part[:, lane : lane + 128]
        if hit is not None:
            weight = jnp.where(hit, -weight, weight)
        return weight.astype(jnp.bfloat16)

    own_all = jnp.concatenate([ref[...] for ref in own], axis=0) if own_count > 1 else own[0][...]
    weights = [[] for _ in own]
    chosen = []
    start = 0
    while start < block_count:
        stop, count = start, 0
        while stop < block_count and count < 256:
            count += blocks[stop].shape[0]
            stop += 1
        block_all = jnp.concatenate([blocks[b][...] for b in range(start, stop)], axis=0)
        chosen.append(block_all)
        dots = lax.dot_general(
            own_all, block_all, (((1,), (1,)), ((), ())), preferred_element_type=jnp.float32
        )
        for a in range(own_count):
            at = 0
            for b in range(start, stop):
                upto = at + blocks[b].shape[0]
                dot = dots[a * own_rows : (a + 1) * own_rows, at:upto]
                weights[a].append(weigh(a, b, dot))
                at = upto
        start = stop
    weight_all = jnp.concatenate([jnp.concatenate(row, axis=1) for row in weights], axis=0)
    block_all = jnp.concatenate(chosen, axis=0)
    term = jnp.dot(weight_all, block_all, preferred_element_type=jnp.float32)
    for a in range(own_count):
        part = term[a * own_rows : (a + 1) * own_rows]
        sums[a][...] = part if first else carried[a][...] + part
    if loss_own:
        losses[...] = loss


def terms(own, blocks, places, targets, pairs, ids, settings, sums, loss_own, loss):
    rows, width = own[0].shape
    kernel = functools.partial(
        terms_kernel,
        len(own),
        len(blocks),
        tuple(places),
        frozenset(pairs),
        sums is None,
        tuple(loss_own),
        loss is None,
    )
    shapes = [jax.ShapeDtypeStruct((rows, width), jnp.float32)] * len(own)
    if loss_own:
        shapes = shapes + [jax.ShapeDtypeStruct((8, 128), jnp.float32)]
    operands = [settings, ids, *own, *blocks, *targets]
    aliases = {}
    if sums is not None:
        aliases = {len(operands) + n: n for n in range(len(own))}
        operands += sums
    if loss_own and loss is not None:
        aliases[len(operands)] = len(own)
        operands.append(loss)
    size = len(own) * rows * sum(block.shape[0] for block in blocks)
    out = pl.pallas_call(
        kernel,
        out_shape=shapes,
        in_specs=[VMEM] * len(operands),
        out_specs=[VMEM] * len(shapes),
        input_output_aliases=aliases,
        cost_estimate=pl.CostEstimate(
            flops=4 * size * width,
            transcendentals=3 * size,
            bytes_accessed=(2 * len(blocks) + 10 * len(own)) * rows * width,
        ),
        compiler_params=PARAMS,
    )(*operands)
    return out[: len(own)], out[len(own)] if loss_own else loss


def factor(count):
    best = 1
    while (best + 1) ** 2 <= count:
        best += 1
    while count % best:
        best -= 1
    return count // best, best


def ring_order(count):
    return list(range(0, count, 2)) + list(range(1, count, 2))[::-1]


def per_device(images, texts, lang_order, position, logit_scale, logit_bias):
    rows, _ = images.shape
    dev_count = lax.axis_size("dev")
    group_count = lax.axis_size("group")
    cores = 2 if group_count % 2 == 0 else 1
    wide = group_count // cores
    slow, fast = factor(dev_count)
    sizes = (wide, cores, slow, fast)

    def permuted(array, dim, move):
        pairs = []
        for index in range(group_count * dev_count):
            place, rest = [], index
            for size in reversed(sizes):
                place.insert(0, rest % size)
                rest //= size
            place[dim] = move(place[dim])
            target = 0
            for size, at in zip(sizes, place):
                target = target * size + at
            pairs.append((index, target))
        return lax.ppermute(array, AXES, pairs)

    def shift(array, dim, by):
        return permuted(array, dim, lambda at: (at + by) % sizes[dim])

    ring = ring_order(slow)
    place_of = [ring.index(at) for at in range(slow)]

    def ring_shift(array):
        return permuted(array, 2, lambda at: ring[(place_of[at] + 1) % slow])

    def exchange(array, dim, by):
        return permuted(array, dim, lambda at: at ^ by)

    dev_index = lax.axis_index("dev")
    slow_index, fast_index = dev_index // fast, dev_index % fast
    offsets = jnp.arange(slow * fast, dtype=jnp.int32)
    ring_index = jnp.array(place_of, dtype=jnp.int32)[slow_index]
    sources = jnp.array(ring, dtype=jnp.int32)[(ring_index - offsets // fast) % slow]
    bases = sources * fast + (fast_index - offsets % fast) % fast
    ids = (rows * bases[:, None] + jnp.arange(rows, dtype=jnp.int32)[None, :]).astype(jnp.int32)
    settings = jnp.concatenate(
        [
            jnp.broadcast_to(logit_scale[:, None], (4, rows)),
            jnp.broadcast_to(logit_bias[:, None], (4, rows)),
        ],
        axis=0,
    )

    txt_half = normalize(texts)
    img_half = normalize(images)

    def spread(block, dim):
        blocks = [block]
        for _ in range(sizes[dim] - 1):
            blocks.append(shift(blocks[-1], dim, 1))
        return blocks

    def with_cores(blocks):
        out = []
        for block in blocks:
            out.append([block] + [shift(block, 1, by) for by in range(1, cores)])
        return out

    img_targets = [position.reshape(1, rows)] * wide
    txt_targets = spread(lang_order.reshape(1, rows), 3)

    def txt_blocks(block):
        return with_cores(spread(block, 3))

    def img_blocks(block):
        return with_cores(spread(block, 0))

    end = slow - 1
    middle = rows // 2
    txt_line, img_line, txt_sets, img_sets = [txt_half], [img_half], [], []
    for step in range(slow):
        if step:
            txt_line.append(ring_shift(txt_line[-1]))
        txt_sets.append(txt_blocks(txt_line[-1]))
        if step < end:
            if step:
                img_line.append(ring_shift(img_line[-1]))
            img_sets.append(img_blocks(img_line[-1]))
    first = ring_shift(img_line[-1][:middle])
    second = ring_shift(img_line[-1][middle:])
    first_set, second_set = img_blocks(first), img_blocks(second)
    img_own = [cores_of[0] for cores_of in img_sets[0]]
    txt_own = [cores_of[0] for cores_of in txt_sets[0]]

    def image_terms(sums, loss, parts, counted=True):
        blocks, places, pairs = [], [], []
        for step, at in parts:
            pairs.append((0, len(blocks)))
            for block in txt_sets[step][at]:
                blocks.append(block)
                places.append((step * fast + at, 0))
        loss_own = range(wide) if counted else ()
        return terms(
            img_own, blocks, places, img_targets, pairs, ids, settings, sums, loss_own, loss,
        )

    def text_terms(sums, loss, parts, loss_own=()):
        blocks, places, pairs = [], [], []
        for cores_of, step, at, offset in parts:
            if at == 0:
                pairs += [(a, len(blocks)) for a in range(fast)]
            for block in cores_of:
                blocks.append(block)
                places.append((step * fast, offset))
        return terms(
            txt_own, blocks, places, txt_targets, pairs, ids, settings, sums, loss_own, loss,
        )

    img_sums = txt_sums = loss = None
    halves = [(first_set, 0), (second_set, middle)]
    for step in range(end):
        parts = [(step, at) for at in range(fast)]
        if step == end - 1:
            parts.append((end, 0))
        img_sums, loss = image_terms(img_sums, loss, parts)
        parts = [(img_sets[step][at], step, at, 0) for at in range(wide)]
        if step == end - 1:
            parts += [(half[0], end, 0, offset) for half, offset in halves]
        counted = range(1, fast) if step == 1 else ()
        txt_sums, loss = text_terms(txt_sums, loss, parts, counted)
    if fast > 1:
        parts = [(end, at) for at in range(1, fast)]
        img_sums, loss = image_terms(img_sums, loss, parts, False)
    if wide > 1:
        parts = [(half[at], end, at, offset) for at in range(1, wide) for half, offset in halves]
        txt_sums, loss = text_terms(txt_sums, loss, parts)

    addends = [loss]
    for dim in (0, 1, 2, 3):
        by = 1
        while by < sizes[dim]:
            loss = sum(addends[1:], addends[0])
            addends = [loss, exchange(loss, dim, by)]
            by = 2 * by
    total = float(rows * dev_count * group_count)
    img_parts = [img_sums[0]] + [shift(img_sums[a], 0, -a) for a in range(1, wide)]
    txt_parts = [txt_sums[0]] + [shift(txt_sums[a], 3, -a) for a in range(1, fast)]
    image_grad = project(images, settings, img_parts, [], 0.0)
    text_grad, loss = project(texts, settings, txt_parts, addends, 1 / (total * total))
    return (image_grad, text_grad, loss)


def solution(mesh):
    return jax.shard_map(
        per_device,
        mesh=mesh,
        in_specs=(
            P(AXES, None),
            P(AXES, None),
            P(AXES),
            P(AXES),
            P(),
            P(),
        ),
        out_specs=(P(AXES, None), P(AXES, None), P()),
        check_vma=False,
    )
```

```python
import functools

import jax
import jax.numpy as jnp
from jax import lax
from jax.experimental import pallas as pl
from jax.experimental.pallas import tpu as pltpu
from jax.sharding import PartitionSpec as P

EPSILON = 1e-06
AXES = ("group", "dev")
VMEM = pl.BlockSpec(memory_space=pltpu.VMEM)
PARAMS = pltpu.CompilerParams(vmem_limit_bytes=16 << 20)


def unit_of(values):
    wide = values.astype(jnp.float32)
    recip = lax.rsqrt(jnp.sum(wide * wide, axis=1, keepdims=True) + EPSILON)
    return wide * recip, recip


def normalize_kernel(values, half):
    half[...] = unit_of(values[...])[0].astype(jnp.bfloat16)


def normalize(values):
    return pl.pallas_call(
        normalize_kernel,
        out_shape=jax.ShapeDtypeStruct(values.shape, jnp.bfloat16),
        in_specs=[VMEM],
        out_specs=VMEM,
        compiler_params=PARAMS,
    )(values)


def project_kernel(count, loss_count, factor, settings, values, *refs):
    parts, losses, out = refs[:count], refs[count : count + loss_count], refs[count + loss_count]
    unit, recip = unit_of(values[...])
    total = parts[0][...]
    for part in parts[1:]:
        total = total + part[...]
    grad = settings[0:1, 0:1] * total
    out[...] = recip * (grad - unit * jnp.sum(unit * grad, axis=1, keepdims=True))
    if loss_count:
        loss = losses[0][...]
        for part in losses[1:]:
            loss = loss + part[...]
        refs[-1][0] = factor * jnp.sum(loss)


def project(values, settings, parts, losses, factor):
    shapes = [jax.ShapeDtypeStruct(values.shape, jnp.float32)]
    specs = [VMEM]
    if losses:
        shapes.append(jax.ShapeDtypeStruct((1,), jnp.float32))
        specs.append(pl.BlockSpec(memory_space=pltpu.SMEM))
    out = pl.pallas_call(
        functools.partial(project_kernel, len(parts), len(losses), factor),
        out_shape=shapes,
        in_specs=[VMEM] * (2 + len(parts) + len(losses)),
        out_specs=specs,
        compiler_params=PARAMS,
    )(settings, values, *parts, *losses)
    return tuple(out) if losses else out[0]


def terms_kernel(
    own_count, block_count, places, pairs, first, loss_own, loss_first, settings, ids, *refs
):
    refs = list(refs)
    own = [refs.pop(0) for _ in range(own_count)]
    blocks = [refs.pop(0) for _ in range(block_count)]
    targets = [refs.pop(0) for _ in range(own_count)]
    carried = [] if first else [refs.pop(0) for _ in range(own_count)]
    loss_in = refs.pop(0) if loss_own and not loss_first else None
    sums = [refs.pop(0) for _ in range(own_count)]
    losses = refs.pop(0) if loss_own else None
    own_rows = own[0].shape[0]
    columns = {}
    for a, _ in sorted(pairs):
        if a not in columns:
            spread = jnp.broadcast_to(targets[a][...], (own_rows, own_rows))
            columns[a] = jnp.transpose(spread)[:, :1]
    loss = None
    if loss_own:
        loss = jnp.zeros((8, 128), jnp.float32) if loss_first else loss_in[...]

    def weigh(a, b, dot):
        nonlocal loss
        block_rows = dot.shape[1]
        logits = settings[0:1, :block_rows] * dot + settings[4:5, :block_rows]
        hit = None
        if (a, b) in pairs:
            at, offset = places[b]
            hit = columns[a] == ids[at : at + 1, offset : offset + block_rows]
            logits = jnp.where(hit, -logits, logits)
        small = jnp.exp(-jnp.abs(logits))
        inverse = 1.0 / (1.0 + small)
        weight = jnp.where(logits >= 0, inverse, small * inverse)
        if a in loss_own:
            part = jnp.maximum(logits, 0.0) + jnp.log1p(small)
            part = jnp.sum(part.reshape(own_rows // 8, 8, block_rows), axis=0)
            for lane in range(0, block_rows, 128):
                loss = loss + part[:, lane : lane + 128]
        if hit is not None:
            weight = jnp.where(hit, -weight, weight)
        return weight.astype(jnp.bfloat16)

    own_all = jnp.concatenate([ref[...] for ref in own], axis=0) if own_count > 1 else own[0][...]
    weights = [[] for _ in own]
    chosen = []
    start = 0
    while start < block_count:
        stop, count = start, 0
        while stop < block_count and count < 256:
            count += blocks[stop].shape[0]
            stop += 1
        block_all = jnp.concatenate([blocks[b][...] for b in range(start, stop)], axis=0)
        chosen.append(block_all)
        dots = lax.dot_general(
            own_all, block_all, (((1,), (1,)), ((), ())), preferred_element_type=jnp.float32
        )
        for a in range(own_count):
            at = 0
            for b in range(start, stop):
                upto = at + blocks[b].shape[0]
                dot = dots[a * own_rows : (a + 1) * own_rows, at:upto]
                weights[a].append(weigh(a, b, dot))
                at = upto
        start = stop
    weight_all = jnp.concatenate([jnp.concatenate(row, axis=1) for row in weights], axis=0)
    block_all = jnp.concatenate(chosen, axis=0)
    term = jnp.dot(weight_all, block_all, preferred_element_type=jnp.float32)
    for a in range(own_count):
        part = term[a * own_rows : (a + 1) * own_rows]
        sums[a][...] = part if first else carried[a][...] + part
    if loss_own:
        losses[...] = loss


def terms(own, blocks, places, targets, pairs, ids, settings, sums, loss_own, loss):
    rows, width = own[0].shape
    kernel = functools.partial(
        terms_kernel,
        len(own),
        len(blocks),
        tuple(places),
        frozenset(pairs),
        sums is None,
        tuple(loss_own),
        loss is None,
    )
    shapes = [jax.ShapeDtypeStruct((rows, width), jnp.float32)] * len(own)
    if loss_own:
        shapes = shapes + [jax.ShapeDtypeStruct((8, 128), jnp.float32)]
    operands = [settings, ids, *own, *blocks, *targets]
    aliases = {}
    if sums is not None:
        aliases = {len(operands) + n: n for n in range(len(own))}
        operands += sums
    if loss_own and loss is not None:
        aliases[len(operands)] = len(own)
        operands.append(loss)
    size = len(own) * rows * sum(block.shape[0] for block in blocks)
    out = pl.pallas_call(
        kernel,
        out_shape=shapes,
        in_specs=[VMEM] * len(operands),
        out_specs=[VMEM] * len(shapes),
        input_output_aliases=aliases,
        cost_estimate=pl.CostEstimate(
            flops=4 * size * width,
            transcendentals=3 * size,
            bytes_accessed=(2 * len(blocks) + 10 * len(own)) * rows * width,
        ),
        compiler_params=PARAMS,
    )(*operands)
    return out[: len(own)], out[len(own)] if loss_own else loss


def factor(count):
    best = 1
    while (best + 1) ** 2 <= count:
        best += 1
    while count % best:
        best -= 1
    return count // best, best


def ring_order(count):
    return list(range(0, count, 2)) + list(range(1, count, 2))[::-1]


def per_device(images, texts, lang_order, position, logit_scale, logit_bias):
    rows, _ = images.shape
    dev_count = lax.axis_size("dev")
    group_count = lax.axis_size("group")
    cores = 2 if group_count % 2 == 0 else 1
    wide = group_count // cores
    slow, fast = factor(dev_count)
    sizes = (wide, cores, slow, fast)

    def permuted(array, dim, move):
        pairs = []
        for index in range(group_count * dev_count):
            place, rest = [], index
            for size in reversed(sizes):
                place.insert(0, rest % size)
                rest //= size
            place[dim] = move(place[dim])
            target = 0
            for size, at in zip(sizes, place):
                target = target * size + at
            pairs.append((index, target))
        return lax.ppermute(array, AXES, pairs)

    def shift(array, dim, by):
        return permuted(array, dim, lambda at: (at + by) % sizes[dim])

    ring = ring_order(slow)
    place_of = [ring.index(at) for at in range(slow)]

    def ring_shift(array):
        return permuted(array, 2, lambda at: ring[(place_of[at] + 1) % slow])

    def exchange(array, dim, by):
        return permuted(array, dim, lambda at: at ^ by)

    dev_index = lax.axis_index("dev")
    slow_index, fast_index = dev_index // fast, dev_index % fast
    offsets = jnp.arange(slow * fast, dtype=jnp.int32)
    odd = slow_index % 2 == 1
    ring_index = jnp.where(odd, slow - 1 - slow_index // 2, slow_index // 2)
    source_index = (ring_index - offsets // fast) % slow
    rising = source_index < (slow + 1) // 2
    sources = jnp.where(rising, 2 * source_index, 2 * (slow - 1 - source_index) + 1)
    bases = sources * fast + (fast_index - offsets % fast) % fast
    ids = (rows * bases[:, None] + jnp.arange(rows, dtype=jnp.int32)[None, :]).astype(jnp.int32)
    settings = jnp.concatenate(
        [
            jnp.broadcast_to(logit_scale[:, None], (4, rows)),
            jnp.broadcast_to(logit_bias[:, None], (4, rows)),
        ],
        axis=0,
    )

    txt_half = normalize(texts)
    img_half = normalize(images)

    def spread(block, dim):
        blocks = [block]
        for _ in range(sizes[dim] - 1):
            blocks.append(shift(blocks[-1], dim, 1))
        return blocks

    def with_cores(blocks):
        out = []
        for block in blocks:
            out.append([block] + [shift(block, 1, by) for by in range(1, cores)])
        return out

    img_targets = [position.reshape(1, rows)] * wide
    txt_targets = spread(lang_order.reshape(1, rows), 3)

    def txt_blocks(block):
        return with_cores(spread(block, 3))

    def img_blocks(block):
        return with_cores(spread(block, 0))

    end = slow - 1
    middle = rows // 2
    txt_line, img_line, txt_sets, img_sets = [txt_half], [img_half], [], []
    for step in range(slow):
        if step == 1:
            block = ring_shift(texts)
            txt_line.append(normalize(block))
        elif step:
            txt_line.append(ring_shift(txt_line[-1]))
        txt_sets.append(txt_blocks(txt_line[-1]))
        if step < end:
            if step == 1:
                block = ring_shift(images)
                img_line.append(normalize(block))
            elif step:
                img_line.append(ring_shift(img_line[-1]))
            img_sets.append(img_blocks(img_line[-1]))
    first = ring_shift(img_line[-1][:middle])
    second = ring_shift(img_line[-1][middle:])
    first_set, second_set = img_blocks(first), img_blocks(second)
    img_own = [cores_of[0] for cores_of in img_sets[0]]
    txt_own = [cores_of[0] for cores_of in txt_sets[0]]

    def image_terms(sums, loss, parts, members, counted):
        blocks, places, pairs = [], [], []
        for step, at in parts:
            if members[0] == 0:
                pairs.append((0, len(blocks)))
            for block in txt_sets[step][at]:
                blocks.append(block)
                places.append((step * fast + at, 0))
        loss_own = range(len(members)) if counted else ()
        own, targets = [img_own[a] for a in members], [img_targets[a] for a in members]
        return terms(own, blocks, places, targets, pairs, ids, settings, sums, loss_own, loss)

    def text_terms(sums, loss, parts, members, counted):
        blocks, places, pairs = [], [], []
        for cores_of, step, at, offset in parts:
            if at == 0:
                pairs += [(a, len(blocks)) for a in range(len(members))]
            for block in cores_of:
                blocks.append(block)
                places.append((step * fast, offset))
        loss_own = range(len(members)) if counted else ()
        own, targets = [txt_own[a] for a in members], [txt_targets[a] for a in members]
        return terms(own, blocks, places, targets, pairs, ids, settings, sums, loss_own, loss)

    img_sums = txt_sums = loss = None
    halves = [(first_set, 0), (second_set, middle)]
    for step in range(end):
        parts = [(step, at) for at in range(fast)]
        img_sums, loss = image_terms(img_sums, loss, parts, range(wide), True)
        parts = [(img_sets[step][at], step, at, 0) for at in range(wide)]
        if step == end - 1:
            parts += [(half[0], end, 0, offset) for half, offset in halves]
        txt_sums, loss = text_terms(txt_sums, loss, parts, range(fast), step == 1)
    parts = [(end, at) for at in range(fast)]
    img_far, _ = image_terms(img_sums[1:], None, parts, range(1, wide), False)
    img_near, _ = image_terms(img_sums[:1], None, parts, range(1), False)
    parts = [(half[at], end, at, offset) for at in range(1, wide) for half, offset in halves]
    txt_far, _ = text_terms(txt_sums[1:], None, parts, range(1, fast), False)
    txt_near, _ = text_terms(txt_sums[:1], None, parts, range(1), False)
    img_sums, txt_sums = [*img_near, *img_far], [*txt_near, *txt_far]

    addends = [loss]
    for dim in (0, 1, 2, 3):
        by = 1
        while by < sizes[dim]:
            loss = sum(addends[1:], addends[0])
            addends = [loss, exchange(loss, dim, by)]
            by = 2 * by
    total = float(rows * dev_count * group_count)
    img_parts = [img_sums[0]] + [shift(img_sums[a], 0, -a) for a in range(1, wide)]
    txt_parts = [txt_sums[0]] + [shift(txt_sums[a], 3, -a) for a in range(1, fast)]
    image_grad = project(images, settings, img_parts, [], 0.0)
    text_grad, loss = project(texts, settings, txt_parts, addends, 1 / (total * total))
    return (image_grad, text_grad, loss)


def solution(mesh):
    return jax.shard_map(
        per_device,
        mesh=mesh,
        in_specs=(
            P(AXES, None),
            P(AXES, None),
            P(AXES),
            P(AXES),
            P(),
            P(),
        ),
        out_specs=(P(AXES, None), P(AXES, None), P()),
        check_vma=False,
    )
```

```python
import functools

import jax
import jax.numpy as jnp
from jax import lax
from jax.experimental import pallas as pl
from jax.experimental.pallas import tpu as pltpu
from jax.sharding import PartitionSpec as P

EPSILON = 1e-06
AXES = ("group", "dev")
VMEM = pl.BlockSpec(memory_space=pltpu.VMEM)
PARAMS = pltpu.CompilerParams(vmem_limit_bytes=16 << 20)


def unit_of(values):
    wide = values.astype(jnp.float32)
    recip = lax.rsqrt(jnp.sum(wide * wide, axis=1, keepdims=True) + EPSILON)
    return wide * recip, recip


def normalize_kernel(values, half):
    half[...] = unit_of(values[...])[0].astype(jnp.bfloat16)


def normalize(values):
    return pl.pallas_call(
        normalize_kernel,
        out_shape=jax.ShapeDtypeStruct(values.shape, jnp.bfloat16),
        in_specs=[VMEM],
        out_specs=VMEM,
        compiler_params=PARAMS,
    )(values)


def project_kernel(count, loss_count, factor, settings, values, *refs):
    parts, losses = refs[:count], refs[count : count + loss_count]
    outs, (held, sems) = refs[count + loss_count : -2], refs[-2:]
    rows = values.shape[0]
    pieces = sems.shape[0]
    copies = []
    for piece in range(pieces):
        some = pl.ds(piece * (rows // pieces), rows // pieces)
        unit, recip = unit_of(values[some, :])
        total = parts[0][some, :]
        for part in parts[1:]:
            total = total + part[some, :]
        grad = settings[0:1, 0:1] * total
        held[some, :] = recip * (grad - unit * jnp.sum(unit * grad, axis=1, keepdims=True))
        copies.append(pltpu.make_async_copy(held.at[some], outs[0].at[some], sems.at[piece]))
        copies[-1].start()
    if loss_count:
        loss = losses[0][...]
        for part in losses[1:]:
            loss = loss + part[...]
        outs[1][0] = factor * jnp.sum(loss)
    for copy in copies:
        copy.wait()


def project(values, settings, parts, losses, factor):
    rows = values.shape[0]
    pieces = 4 if rows % 64 == 0 else 1
    shapes = [jax.ShapeDtypeStruct(values.shape, jnp.float32)]
    specs = [pl.BlockSpec(memory_space=pl.ANY)]
    if losses:
        shapes.append(jax.ShapeDtypeStruct((1,), jnp.float32))
        specs.append(pl.BlockSpec(memory_space=pltpu.SMEM))
    out = pl.pallas_call(
        functools.partial(project_kernel, len(parts), len(losses), factor),
        out_shape=shapes,
        in_specs=[VMEM] * (2 + len(parts) + len(losses)),
        out_specs=specs,
        scratch_shapes=[
            pltpu.VMEM(values.shape, jnp.float32),
            pltpu.SemaphoreType.DMA((pieces,)),
        ],
        compiler_params=PARAMS,
    )(settings, values, *parts, *losses)
    return tuple(out) if losses else out[0]


def terms_kernel(
    own_count, block_count, places, pairs, first, loss_own, loss_first, settings, ids, *refs
):
    refs = list(refs)
    own = [refs.pop(0) for _ in range(own_count)]
    blocks = [refs.pop(0) for _ in range(block_count)]
    targets = [refs.pop(0) for _ in range(own_count)]
    carried = [] if first else [refs.pop(0) for _ in range(own_count)]
    loss_in = refs.pop(0) if loss_own and not loss_first else None
    sums = [refs.pop(0) for _ in range(own_count)]
    losses = refs.pop(0) if loss_own else None
    own_rows = own[0].shape[0]
    columns = {}
    for a, _ in sorted(pairs):
        if a not in columns:
            spread = jnp.broadcast_to(targets[a][...], (own_rows, own_rows))
            columns[a] = jnp.transpose(spread)[:, :1]
    loss = None
    if loss_own:
        loss = jnp.zeros((8, 128), jnp.float32) if loss_first else loss_in[...]

    def weigh(a, b, dot):
        nonlocal loss
        block_rows = dot.shape[1]
        logits = settings[0:1, :block_rows] * dot + settings[4:5, :block_rows]
        hit = None
        if (a, b) in pairs:
            at, offset = places[b]
            hit = columns[a] == ids[at : at + 1, offset : offset + block_rows]
            logits = jnp.where(hit, -logits, logits)
        small = jnp.exp(-jnp.abs(logits))
        inverse = 1.0 / (1.0 + small)
        weight = jnp.where(logits >= 0, inverse, small * inverse)
        if a in loss_own:
            part = jnp.maximum(logits, 0.0) + jnp.log1p(small)
            part = jnp.sum(part.reshape(own_rows // 8, 8, block_rows), axis=0)
            for lane in range(0, block_rows, 128):
                loss = loss + part[:, lane : lane + 128]
        if hit is not None:
            weight = jnp.where(hit, -weight, weight)
        return weight.astype(jnp.bfloat16)

    own_all = jnp.concatenate([ref[...] for ref in own], axis=0) if own_count > 1 else own[0][...]
    weights = [[] for _ in own]
    chosen = []
    start = 0
    while start < block_count:
        stop, count = start, 0
        while stop < block_count and count < 256:
            count += blocks[stop].shape[0]
            stop += 1
        block_all = jnp.concatenate([blocks[b][...] for b in range(start, stop)], axis=0)
        chosen.append(block_all)
        dots = lax.dot_general(
            own_all, block_all, (((1,), (1,)), ((), ())), preferred_element_type=jnp.float32
        )
        for a in range(own_count):
            at = 0
            for b in range(start, stop):
                upto = at + blocks[b].shape[0]
                dot = dots[a * own_rows : (a + 1) * own_rows, at:upto]
                weights[a].append(weigh(a, b, dot))
                at = upto
        start = stop
    weight_all = jnp.concatenate([jnp.concatenate(row, axis=1) for row in weights], axis=0)
    block_all = jnp.concatenate(chosen, axis=0)
    term = jnp.dot(weight_all, block_all, preferred_element_type=jnp.float32)
    for a in range(own_count):
        part = term[a * own_rows : (a + 1) * own_rows]
        sums[a][...] = part if first else carried[a][...] + part
    if loss_own:
        losses[...] = loss


def terms(own, blocks, places, targets, pairs, ids, settings, sums, loss_own, loss):
    rows, width = own[0].shape
    kernel = functools.partial(
        terms_kernel,
        len(own),
        len(blocks),
        tuple(places),
        frozenset(pairs),
        sums is None,
        tuple(loss_own),
        loss is None,
    )
    shapes = [jax.ShapeDtypeStruct((rows, width), jnp.float32)] * len(own)
    if loss_own:
        shapes = shapes + [jax.ShapeDtypeStruct((8, 128), jnp.float32)]
    operands = [settings, ids, *own, *blocks, *targets]
    aliases = {}
    if sums is not None:
        aliases = {len(operands) + n: n for n in range(len(own))}
        operands += sums
    if loss_own and loss is not None:
        aliases[len(operands)] = len(own)
        operands.append(loss)
    size = len(own) * rows * sum(block.shape[0] for block in blocks)
    out = pl.pallas_call(
        kernel,
        out_shape=shapes,
        in_specs=[VMEM] * len(operands),
        out_specs=[VMEM] * len(shapes),
        input_output_aliases=aliases,
        cost_estimate=pl.CostEstimate(
            flops=4 * size * width,
            transcendentals=3 * size,
            bytes_accessed=(2 * len(blocks) + 10 * len(own)) * rows * width,
        ),
        compiler_params=PARAMS,
    )(*operands)
    return out[: len(own)], out[len(own)] if loss_own else loss


def factor(count):
    best = 1
    while (best + 1) ** 2 <= count:
        best += 1
    while count % best:
        best -= 1
    return count // best, best


def ring_order(count):
    return list(range(0, count, 2)) + list(range(1, count, 2))[::-1]


def per_device(images, texts, lang_order, position, logit_scale, logit_bias):
    rows, _ = images.shape
    dev_count = lax.axis_size("dev")
    group_count = lax.axis_size("group")
    cores = 2 if group_count % 2 == 0 else 1
    wide = group_count // cores
    slow, fast = factor(dev_count)
    sizes = (wide, cores, slow, fast)

    def permuted(array, dim, move):
        pairs = []
        for index in range(group_count * dev_count):
            place, rest = [], index
            for size in reversed(sizes):
                place.insert(0, rest % size)
                rest //= size
            place[dim] = move(place[dim])
            target = 0
            for size, at in zip(sizes, place):
                target = target * size + at
            pairs.append((index, target))
        return lax.ppermute(array, AXES, pairs)

    def shift(array, dim, by):
        return permuted(array, dim, lambda at: (at + by) % sizes[dim])

    ring = ring_order(slow)
    place_of = [ring.index(at) for at in range(slow)]

    def ring_shift(array):
        return permuted(array, 2, lambda at: ring[(place_of[at] + 1) % slow])

    def exchange(array, dim, by):
        return permuted(array, dim, lambda at: at ^ by)

    dev_index = lax.axis_index("dev")
    slow_index, fast_index = dev_index // fast, dev_index % fast
    offsets = jnp.arange(slow * fast, dtype=jnp.int32)
    odd = slow_index % 2 == 1
    ring_index = jnp.where(odd, slow - 1 - slow_index // 2, slow_index // 2)
    source_index = (ring_index - offsets // fast) % slow
    rising = source_index < (slow + 1) // 2
    sources = jnp.where(rising, 2 * source_index, 2 * (slow - 1 - source_index) + 1)
    bases = sources * fast + (fast_index - offsets % fast) % fast
    ids = (rows * bases[:, None] + jnp.arange(rows, dtype=jnp.int32)[None, :]).astype(jnp.int32)
    settings = jnp.concatenate(
        [
            jnp.broadcast_to(logit_scale[:, None], (4, rows)),
            jnp.broadcast_to(logit_bias[:, None], (4, rows)),
        ],
        axis=0,
    )

    txt_half = normalize(texts)
    img_half = normalize(images)

    def spread(block, dim):
        blocks = [block]
        for _ in range(sizes[dim] - 1):
            blocks.append(shift(blocks[-1], dim, 1))
        return blocks

    def with_cores(blocks):
        out = []
        for block in blocks:
            out.append([block] + [shift(block, 1, by) for by in range(1, cores)])
        return out

    img_targets = [position.reshape(1, rows)] * wide
    txt_targets = spread(lang_order.reshape(1, rows), 3)

    def txt_blocks(block):
        return with_cores(spread(block, 3))

    def img_blocks(block):
        return with_cores(spread(block, 0))

    end = slow - 1
    middle = rows // 2
    txt_line, img_line, txt_sets, img_sets = [txt_half], [img_half], [], []
    for step in range(slow):
        if step == 1:
            block = ring_shift(texts)
            txt_line.append(normalize(block))
        elif step:
            txt_line.append(ring_shift(txt_line[-1]))
        txt_sets.append(txt_blocks(txt_line[-1]))
        if step < end:
            if step == 1:
                block = ring_shift(images)
                img_line.append(normalize(block))
            elif step:
                img_line.append(ring_shift(img_line[-1]))
            img_sets.append(img_blocks(img_line[-1]))
    first = ring_shift(img_line[-1][:middle])
    second = ring_shift(img_line[-1][middle:])
    first_set, second_set = img_blocks(first), img_blocks(second)
    img_own = [cores_of[0] for cores_of in img_sets[0]]
    txt_own = [cores_of[0] for cores_of in txt_sets[0]]

    def image_terms(sums, loss, parts, members, counted):
        blocks, places, pairs = [], [], []
        for step, at in parts:
            if members[0] == 0:
                pairs.append((0, len(blocks)))
            for block in txt_sets[step][at]:
                blocks.append(block)
                places.append((step * fast + at, 0))
        loss_own = range(len(members)) if counted else ()
        own, targets = [img_own[a] for a in members], [img_targets[a] for a in members]
        return terms(own, blocks, places, targets, pairs, ids, settings, sums, loss_own, loss)

    def text_terms(sums, loss, parts, members, counted):
        blocks, places, pairs = [], [], []
        for cores_of, step, at, offset in parts:
            if at == 0:
                pairs += [(a, len(blocks)) for a in range(len(members))]
            for block in cores_of:
                blocks.append(block)
                places.append((step * fast, offset))
        loss_own = range(len(members)) if counted else ()
        own, targets = [txt_own[a] for a in members], [txt_targets[a] for a in members]
        return terms(own, blocks, places, targets, pairs, ids, settings, sums, loss_own, loss)

    img_sums = txt_sums = loss = None
    halves = [(first_set, 0), (second_set, middle)]
    for step in range(end):
        parts = [(step, at) for at in range(fast)]
        img_sums, loss = image_terms(img_sums, loss, parts, range(wide), True)
        parts = [(img_sets[step][at], step, at, 0) for at in range(wide)]
        if step == end - 1:
            parts.append((first_set[0], end, 0, 0))
        txt_sums, loss = text_terms(txt_sums, loss, parts, range(fast), step == 1)
    parts = [(end, at) for at in range(fast)]
    img_far, _ = image_terms(img_sums[1:], None, parts, range(1, wide), False)
    img_near, _ = image_terms(img_sums[:1], None, parts, range(1), False)
    parts = [(second_set[0], end, 0, middle)]
    parts += [(half[at], end, at, offset) for at in range(1, wide) for half, offset in halves]
    txt_far, _ = text_terms(txt_sums[1:], None, parts, range(1, fast), False)
    txt_near, _ = text_terms(txt_sums[:1], None, parts, range(1), False)
    img_sums, txt_sums = [*img_near, *img_far], [*txt_near, *txt_far]

    addends = [loss]
    for dim in (0, 1, 2, 3):
        by = 1
        while by < sizes[dim]:
            loss = sum(addends[1:], addends[0])
            addends = [loss, exchange(loss, dim, by)]
            by = 2 * by
    total = float(rows * dev_count * group_count)
    img_parts = [img_sums[0]] + [shift(img_sums[a], 0, -a) for a in range(1, wide)]
    txt_parts = [txt_sums[0]] + [shift(txt_sums[a], 3, -a) for a in range(1, fast)]
    image_grad = project(images, settings, img_parts, [], 0.0)
    text_grad, loss = project(texts, settings, txt_parts, addends, 1 / (total * total))
    return (image_grad, text_grad, loss)


def solution(mesh):
    return jax.shard_map(
        per_device,
        mesh=mesh,
        in_specs=(
            P(AXES, None),
            P(AXES, None),
            P(AXES),
            P(AXES),
            P(),
            P(),
        ),
        out_specs=(P(AXES, None), P(AXES, None), P()),
        check_vma=False,
    )
```

```python
import functools

import jax
import jax.numpy as jnp
from jax import lax
from jax.experimental import pallas as pl
from jax.experimental.pallas import tpu as pltpu
from jax.sharding import PartitionSpec as P

EPSILON = 1e-06
AXES = ("group", "dev")
VMEM = pl.BlockSpec(memory_space=pltpu.VMEM)
PARAMS = pltpu.CompilerParams(vmem_limit_bytes=16 << 20)


def unit_of(values):
    wide = values.astype(jnp.float32)
    recip = lax.rsqrt(jnp.sum(wide * wide, axis=1, keepdims=True) + EPSILON)
    return wide * recip, recip


def normalize_kernel(values, half):
    half[...] = unit_of(values[...])[0].astype(jnp.bfloat16)


def normalize(values):
    return pl.pallas_call(
        normalize_kernel,
        out_shape=jax.ShapeDtypeStruct(values.shape, jnp.bfloat16),
        in_specs=[VMEM],
        out_specs=VMEM,
        compiler_params=PARAMS,
    )(values)


def project_kernel(count, loss_count, factor, settings, values, *refs):
    parts, losses, out = refs[:count], refs[count : count + loss_count], refs[count + loss_count]
    unit, recip = unit_of(values[...])
    total = parts[0][...]
    for part in parts[1:]:
        total = total + part[...]
    grad = settings[0:1, 0:1] * total
    out[...] = recip * (grad - unit * jnp.sum(unit * grad, axis=1, keepdims=True))
    if loss_count:
        loss = losses[0][...]
        for part in losses[1:]:
            loss = loss + part[...]
        refs[-1][0] = factor * jnp.sum(loss)


def project(values, settings, parts, losses, factor):
    shapes = [jax.ShapeDtypeStruct(values.shape, jnp.float32)]
    specs = [VMEM]
    if losses:
        shapes.append(jax.ShapeDtypeStruct((1,), jnp.float32))
        specs.append(pl.BlockSpec(memory_space=pltpu.SMEM))
    out = pl.pallas_call(
        functools.partial(project_kernel, len(parts), len(losses), factor),
        out_shape=shapes,
        in_specs=[VMEM] * (2 + len(parts) + len(losses)),
        out_specs=specs,
        compiler_params=PARAMS,
    )(settings, values, *parts, *losses)
    return tuple(out) if losses else out[0]


def terms_kernel(
    own_count, block_count, places, pairs, first, loss_own, loss_first, settings, ids, *refs
):
    refs = list(refs)
    own = [refs.pop(0) for _ in range(own_count)]
    blocks = [refs.pop(0) for _ in range(block_count)]
    targets = [refs.pop(0) for _ in range(own_count)]
    carried = [] if first else [refs.pop(0) for _ in range(own_count)]
    loss_in = refs.pop(0) if loss_own and not loss_first else None
    sums = [refs.pop(0) for _ in range(own_count)]
    losses = refs.pop(0) if loss_own else None
    own_rows = own[0].shape[0]
    columns = {}
    for a, _ in sorted(pairs):
        if a not in columns:
            spread = jnp.broadcast_to(targets[a][...], (own_rows, own_rows))
            columns[a] = jnp.transpose(spread)[:, :1]
    loss = None
    if loss_own:
        loss = jnp.zeros((8, 128), jnp.float32) if loss_first else loss_in[...]

    def weigh(a, b, dot):
        nonlocal loss
        block_rows = dot.shape[1]
        logits = settings[0:1, :block_rows] * dot + settings[4:5, :block_rows]
        hit = None
        if (a, b) in pairs:
            at, offset = places[b]
            hit = columns[a] == ids[at : at + 1, offset : offset + block_rows]
            logits = jnp.where(hit, -logits, logits)
        small = jnp.exp(-jnp.abs(logits))
        inverse = 1.0 / (1.0 + small)
        weight = jnp.where(logits >= 0, inverse, small * inverse)
        if a in loss_own:
            part = jnp.maximum(logits, 0.0) + jnp.log1p(small)
            part = jnp.sum(part.reshape(own_rows // 8, 8, block_rows), axis=0)
            for lane in range(0, block_rows, 128):
                loss = loss + part[:, lane : lane + 128]
        if hit is not None:
            weight = jnp.where(hit, -weight, weight)
        return weight.astype(jnp.bfloat16)

    own_all = jnp.concatenate([ref[...] for ref in own], axis=0) if own_count > 1 else own[0][...]
    weights = [[] for _ in own]
    chosen = []
    start = 0
    while start < block_count:
        stop, count = start, 0
        while stop < block_count and count < 256:
            count += blocks[stop].shape[0]
            stop += 1
        block_all = jnp.concatenate([blocks[b][...] for b in range(start, stop)], axis=0)
        chosen.append(block_all)
        dots = lax.dot_general(
            own_all, block_all, (((1,), (1,)), ((), ())), preferred_element_type=jnp.float32
        )
        for a in range(own_count):
            at = 0
            for b in range(start, stop):
                upto = at + blocks[b].shape[0]
                dot = dots[a * own_rows : (a + 1) * own_rows, at:upto]
                weights[a].append(weigh(a, b, dot))
                at = upto
        start = stop
    weight_all = jnp.concatenate([jnp.concatenate(row, axis=1) for row in weights], axis=0)
    block_all = jnp.concatenate(chosen, axis=0)
    term = jnp.dot(weight_all, block_all, preferred_element_type=jnp.float32)
    for a in range(own_count):
        part = term[a * own_rows : (a + 1) * own_rows]
        sums[a][...] = part if first else carried[a][...] + part
    if loss_own:
        losses[...] = loss


def terms(own, blocks, places, targets, pairs, ids, settings, sums, loss_own, loss):
    rows, width = own[0].shape
    kernel = functools.partial(
        terms_kernel,
        len(own),
        len(blocks),
        tuple(places),
        frozenset(pairs),
        sums is None,
        tuple(loss_own),
        loss is None,
    )
    shapes = [jax.ShapeDtypeStruct((rows, width), jnp.float32)] * len(own)
    if loss_own:
        shapes = shapes + [jax.ShapeDtypeStruct((8, 128), jnp.float32)]
    operands = [settings, ids, *own, *blocks, *targets]
    aliases = {}
    if sums is not None:
        aliases = {len(operands) + n: n for n in range(len(own))}
        operands += sums
    if loss_own and loss is not None:
        aliases[len(operands)] = len(own)
        operands.append(loss)
    size = len(own) * rows * sum(block.shape[0] for block in blocks)
    out = pl.pallas_call(
        kernel,
        out_shape=shapes,
        in_specs=[VMEM] * len(operands),
        out_specs=[VMEM] * len(shapes),
        input_output_aliases=aliases,
        cost_estimate=pl.CostEstimate(
            flops=4 * size * width,
            transcendentals=3 * size,
            bytes_accessed=(2 * len(blocks) + 10 * len(own)) * rows * width,
        ),
        compiler_params=PARAMS,
    )(*operands)
    return out[: len(own)], out[len(own)] if loss_own else loss


def factor(count):
    best = 1
    while (best + 1) ** 2 <= count:
        best += 1
    while count % best:
        best -= 1
    return count // best, best


def ring_order(count):
    return list(range(0, count, 2)) + list(range(1, count, 2))[::-1]


def per_device(images, texts, lang_order, position, logit_scale, logit_bias):
    rows, _ = images.shape
    dev_count = lax.axis_size("dev")
    group_count = lax.axis_size("group")
    cores = 2 if group_count % 2 == 0 else 1
    wide = group_count // cores
    slow, fast = factor(dev_count)
    sizes = (wide, cores, slow, fast)

    def permuted(array, dim, move):
        pairs = []
        for index in range(group_count * dev_count):
            place, rest = [], index
            for size in reversed(sizes):
                place.insert(0, rest % size)
                rest //= size
            place[dim] = move(place[dim])
            target = 0
            for size, at in zip(sizes, place):
                target = target * size + at
            pairs.append((index, target))
        return lax.ppermute(array, AXES, pairs)

    def shift(array, dim, by):
        return permuted(array, dim, lambda at: (at + by) % sizes[dim])

    ring = ring_order(slow)
    place_of = [ring.index(at) for at in range(slow)]

    def ring_shift(array):
        return permuted(array, 2, lambda at: ring[(place_of[at] + 1) % slow])

    def exchange(array, dim, by):
        return permuted(array, dim, lambda at: at ^ by)

    dev_index = lax.axis_index("dev")
    slow_index, fast_index = dev_index // fast, dev_index % fast
    offsets = jnp.arange(slow * fast, dtype=jnp.int32)
    odd = slow_index % 2 == 1
    ring_index = jnp.where(odd, slow - 1 - slow_index // 2, slow_index // 2)
    source_index = (ring_index - offsets // fast) % slow
    rising = source_index < (slow + 1) // 2
    sources = jnp.where(rising, 2 * source_index, 2 * (slow - 1 - source_index) + 1)
    bases = sources * fast + (fast_index - offsets % fast) % fast
    ids = (rows * bases[:, None] + jnp.arange(rows, dtype=jnp.int32)[None, :]).astype(jnp.int32)
    settings = jnp.concatenate(
        [
            jnp.broadcast_to(logit_scale[:, None], (4, rows)),
            jnp.broadcast_to(logit_bias[:, None], (4, rows)),
        ],
        axis=0,
    )

    txt_half = normalize(texts)
    img_half = normalize(images)

    def spread(block, dim):
        blocks = [block]
        for _ in range(sizes[dim] - 1):
            blocks.append(shift(blocks[-1], dim, 1))
        return blocks

    def with_cores(blocks):
        out = []
        for block in blocks:
            out.append([block] + [shift(block, 1, by) for by in range(1, cores)])
        return out

    img_targets = [position.reshape(1, rows)] * wide
    txt_targets = spread(lang_order.reshape(1, rows), 3)

    def txt_blocks(block):
        return with_cores(spread(block, 3))

    def img_blocks(block):
        return with_cores(spread(block, 0))

    end = slow - 1
    middle = rows // 2
    txt_line, img_line, txt_sets, img_sets = [txt_half], [img_half], [], []
    for step in range(slow):
        if step == 1:
            block = ring_shift(texts)
            txt_line.append(normalize(block))
        elif step:
            txt_line.append(ring_shift(txt_line[-1]))
        txt_sets.append(txt_blocks(txt_line[-1]))
        if step < end:
            if step == 1:
                block = ring_shift(images)
                img_line.append(normalize(block))
            elif step:
                img_line.append(ring_shift(img_line[-1]))
            img_sets.append(img_blocks(img_line[-1]))
    first = ring_shift(img_line[-1][:middle])
    second = ring_shift(img_line[-1][middle:])
    first_set, second_set = img_blocks(first), img_blocks(second)
    img_own = [cores_of[0] for cores_of in img_sets[0]]
    txt_own = [cores_of[0] for cores_of in txt_sets[0]]

    def image_terms(sums, loss, parts, members, counted):
        blocks, places, pairs = [], [], []
        for step, at in parts:
            if members[0] == 0:
                pairs.append((0, len(blocks)))
            for block in txt_sets[step][at]:
                blocks.append(block)
                places.append((step * fast + at, 0))
        loss_own = range(len(members)) if counted else ()
        own, targets = [img_own[a] for a in members], [img_targets[a] for a in members]
        return terms(own, blocks, places, targets, pairs, ids, settings, sums, loss_own, loss)

    def text_terms(sums, loss, parts, members, counted):
        blocks, places, pairs = [], [], []
        for cores_of, step, at, offset in parts:
            if at == 0:
                pairs += [(a, len(blocks)) for a in range(len(members))]
            for block in cores_of:
                blocks.append(block)
                places.append((step * fast, offset))
        loss_own = range(len(members)) if counted else ()
        own, targets = [txt_own[a] for a in members], [txt_targets[a] for a in members]
        return terms(own, blocks, places, targets, pairs, ids, settings, sums, loss_own, loss)

    img_sums = txt_sums = loss = None
    halves = [(first_set, 0), (second_set, middle)]
    for step in range(end):
        parts = [(step, at) for at in range(fast)]
        img_sums, loss = image_terms(img_sums, loss, parts, range(wide), True)
        parts = [(img_sets[step][at], step, at, 0) for at in range(wide)]
        if step == end - 1:
            parts.append((first_set[0], end, 0, 0))
        txt_sums, loss = text_terms(txt_sums, loss, parts, range(fast), step == 1)
    parts = [(end, at) for at in range(fast)]
    img_far, _ = image_terms(img_sums[1:], None, parts, range(1, wide), False)
    img_near, _ = image_terms(img_sums[:1], None, parts, range(1), False)
    parts = [(second_set[0], end, 0, middle)]
    parts += [(half[at], end, at, offset) for at in range(1, wide) for half, offset in halves]
    txt_far, _ = text_terms(txt_sums[1:], None, parts, range(1, fast), False)
    txt_near, _ = text_terms(txt_sums[:1], None, parts, range(1), False)
    img_sums, txt_sums = [*img_near, *img_far], [*txt_near, *txt_far]

    addends = [loss]
    for dim in (0, 1, 2, 3):
        by = 1
        while by < sizes[dim]:
            loss = sum(addends[1:], addends[0])
            addends = [loss, exchange(loss, dim, by)]
            by = 2 * by
    total = float(rows * dev_count * group_count)
    img_parts = [img_sums[0]] + [shift(img_sums[a], 0, -a) for a in range(1, wide)]
    txt_parts = [txt_sums[0]] + [shift(txt_sums[a], 3, -a) for a in range(1, fast)]
    image_grad = project(images, settings, img_parts, [], 0.0)
    text_grad, loss = project(texts, settings, txt_parts, addends, 1 / (total * total))
    return (image_grad, text_grad, loss)


def solution(mesh):
    return jax.shard_map(
        per_device,
        mesh=mesh,
        in_specs=(
            P(AXES, None),
            P(AXES, None),
            P(AXES),
            P(AXES),
            P(),
            P(),
        ),
        out_specs=(P(AXES, None), P(AXES, None), P()),
        check_vma=False,
    )
```

```python
import functools

import jax
import jax.numpy as jnp
from jax import lax
from jax.experimental import pallas as pl
from jax.experimental.pallas import tpu as pltpu
from jax.sharding import PartitionSpec as P

EPSILON = 1e-06
AXES = ("group", "dev")
VMEM = pl.BlockSpec(memory_space=pltpu.VMEM)
PARAMS = pltpu.CompilerParams(vmem_limit_bytes=16 << 20)


def unit_of(values):
    wide = values.astype(jnp.float32)
    recip = lax.rsqrt(jnp.sum(wide * wide, axis=1, keepdims=True) + EPSILON)
    return wide * recip, recip


def normalize_kernel(values, half):
    half[...] = unit_of(values[...])[0].astype(jnp.bfloat16)


def normalize(values):
    return pl.pallas_call(
        normalize_kernel,
        out_shape=jax.ShapeDtypeStruct(values.shape, jnp.bfloat16),
        in_specs=[VMEM],
        out_specs=VMEM,
        compiler_params=PARAMS,
    )(values)


def project_kernel(count, loss_count, factor, settings, values, *refs):
    parts, losses, out = refs[:count], refs[count : count + loss_count], refs[count + loss_count]
    unit, recip = unit_of(values[...])
    total = parts[0][...]
    for part in parts[1:]:
        total = total + part[...]
    grad = settings[0:1, 0:1] * total
    out[...] = recip * (grad - unit * jnp.sum(unit * grad, axis=1, keepdims=True))
    if loss_count:
        loss = losses[0][...]
        for part in losses[1:]:
            loss = loss + part[...]
        refs[-1][0] = factor * jnp.sum(loss)


def project(values, settings, parts, losses, factor):
    shapes = [jax.ShapeDtypeStruct(values.shape, jnp.float32)]
    specs = [VMEM]
    if losses:
        shapes.append(jax.ShapeDtypeStruct((1,), jnp.float32))
        specs.append(pl.BlockSpec(memory_space=pltpu.SMEM))
    out = pl.pallas_call(
        functools.partial(project_kernel, len(parts), len(losses), factor),
        out_shape=shapes,
        in_specs=[VMEM] * (2 + len(parts) + len(losses)),
        out_specs=specs,
        compiler_params=PARAMS,
    )(settings, values, *parts, *losses)
    return tuple(out) if losses else out[0]


def terms_kernel(
    own_count, block_count, places, pairs, first, loss_own, loss_first, settings, ids, *refs
):
    refs = list(refs)
    own = [refs.pop(0) for _ in range(own_count)]
    blocks = [refs.pop(0) for _ in range(block_count)]
    targets = [refs.pop(0) for _ in range(own_count)]
    carried = [] if first else [refs.pop(0) for _ in range(own_count)]
    loss_in = refs.pop(0) if loss_own and not loss_first else None
    sums = [refs.pop(0) for _ in range(own_count)]
    losses = refs.pop(0) if loss_own else None
    own_rows = own[0].shape[0]
    columns = {}
    for a, _ in sorted(pairs):
        if a not in columns:
            spread = jnp.broadcast_to(targets[a][...], (own_rows, own_rows))
            columns[a] = jnp.transpose(spread)[:, :1]
    loss = None
    if loss_own:
        loss = jnp.zeros((8, 128), jnp.float32) if loss_first else loss_in[...]

    def weigh(a, b, dot):
        nonlocal loss
        block_rows = dot.shape[1]
        logits = settings[0:1, :block_rows] * dot + settings[4:5, :block_rows]
        hit = None
        if (a, b) in pairs:
            at, offset = places[b]
            hit = columns[a] == ids[at : at + 1, offset : offset + block_rows]
            logits = jnp.where(hit, -logits, logits)
        small = jnp.exp(-jnp.abs(logits))
        inverse = 1.0 / (1.0 + small)
        weight = jnp.where(logits >= 0, inverse, small * inverse)
        if a in loss_own:
            part = jnp.maximum(logits, 0.0) + jnp.log1p(small)
            part = jnp.sum(part.reshape(own_rows // 8, 8, block_rows), axis=0)
            for lane in range(0, block_rows, 128):
                loss = loss + part[:, lane : lane + 128]
        if hit is not None:
            weight = jnp.where(hit, -weight, weight)
        return weight.astype(jnp.bfloat16)

    own_all = jnp.concatenate([ref[...] for ref in own], axis=0) if own_count > 1 else own[0][...]
    weights = [[] for _ in own]
    chosen = []
    start = 0
    while start < block_count:
        stop, count = start, 0
        while stop < block_count and count < 256:
            count += blocks[stop].shape[0]
            stop += 1
        block_all = jnp.concatenate([blocks[b][...] for b in range(start, stop)], axis=0)
        chosen.append(block_all)
        dots = lax.dot_general(
            own_all, block_all, (((1,), (1,)), ((), ())), preferred_element_type=jnp.float32
        )
        for a in range(own_count):
            at = 0
            for b in range(start, stop):
                upto = at + blocks[b].shape[0]
                dot = dots[a * own_rows : (a + 1) * own_rows, at:upto]
                weights[a].append(weigh(a, b, dot))
                at = upto
        start = stop
    weight_all = jnp.concatenate([jnp.concatenate(row, axis=1) for row in weights], axis=0)
    block_all = jnp.concatenate(chosen, axis=0)
    term = jnp.dot(weight_all, block_all, preferred_element_type=jnp.float32)
    for a in range(own_count):
        part = term[a * own_rows : (a + 1) * own_rows]
        sums[a][...] = part if first else carried[a][...] + part
    if loss_own:
        losses[...] = loss


def terms(own, blocks, places, targets, pairs, ids, settings, sums, loss_own, loss):
    rows, width = own[0].shape
    kernel = functools.partial(
        terms_kernel,
        len(own),
        len(blocks),
        tuple(places),
        frozenset(pairs),
        sums is None,
        tuple(loss_own),
        loss is None,
    )
    shapes = [jax.ShapeDtypeStruct((rows, width), jnp.float32)] * len(own)
    if loss_own:
        shapes = shapes + [jax.ShapeDtypeStruct((8, 128), jnp.float32)]
    operands = [settings, ids, *own, *blocks, *targets]
    aliases = {}
    if sums is not None:
        aliases = {len(operands) + n: n for n in range(len(own))}
        operands += sums
    if loss_own and loss is not None:
        aliases[len(operands)] = len(own)
        operands.append(loss)
    size = len(own) * rows * sum(block.shape[0] for block in blocks)
    out = pl.pallas_call(
        kernel,
        out_shape=shapes,
        in_specs=[VMEM] * len(operands),
        out_specs=[VMEM] * len(shapes),
        input_output_aliases=aliases,
        cost_estimate=pl.CostEstimate(
            flops=4 * size * width,
            transcendentals=3 * size,
            bytes_accessed=(2 * len(blocks) + 10 * len(own)) * rows * width,
        ),
        compiler_params=PARAMS,
    )(*operands)
    return out[: len(own)], out[len(own)] if loss_own else loss


def factor(count):
    best = 1
    while (best + 1) ** 2 <= count:
        best += 1
    while count % best:
        best -= 1
    return count // best, best


def ring_order(count):
    return list(range(0, count, 2)) + list(range(1, count, 2))[::-1]


def per_device(images, texts, lang_order, position, logit_scale, logit_bias):
    rows, _ = images.shape
    dev_count = lax.axis_size("dev")
    group_count = lax.axis_size("group")
    cores = 2 if group_count % 2 == 0 else 1
    wide = group_count // cores
    slow, fast = factor(dev_count)
    sizes = (wide, cores, slow, fast)

    def permuted(array, dim, move):
        pairs = []
        for index in range(group_count * dev_count):
            place, rest = [], index
            for size in reversed(sizes):
                place.insert(0, rest % size)
                rest //= size
            place[dim] = move(place[dim])
            target = 0
            for size, at in zip(sizes, place):
                target = target * size + at
            pairs.append((index, target))
        return lax.ppermute(array, AXES, pairs)

    def shift(array, dim, by):
        return permuted(array, dim, lambda at: (at + by) % sizes[dim])

    ring = ring_order(slow)
    place_of = [ring.index(at) for at in range(slow)]

    def ring_shift(array):
        return permuted(array, 2, lambda at: ring[(place_of[at] + 1) % slow])

    def exchange(array, dim, by):
        return permuted(array, dim, lambda at: at ^ by)

    dev_index = lax.axis_index("dev")
    slow_index, fast_index = dev_index // fast, dev_index % fast
    offsets = jnp.arange(slow * fast, dtype=jnp.int32)
    odd = slow_index % 2 == 1
    ring_index = jnp.where(odd, slow - 1 - slow_index // 2, slow_index // 2)
    source_index = (ring_index - offsets // fast) % slow
    rising = source_index < (slow + 1) // 2
    sources = jnp.where(rising, 2 * source_index, 2 * (slow - 1 - source_index) + 1)
    bases = sources * fast + (fast_index - offsets % fast) % fast
    ids = (rows * bases[:, None] + jnp.arange(rows, dtype=jnp.int32)[None, :]).astype(jnp.int32)
    settings = jnp.concatenate(
        [
            jnp.broadcast_to(logit_scale[:, None], (4, rows)),
            jnp.broadcast_to(logit_bias[:, None], (4, rows)),
        ],
        axis=0,
    )

    txt_half = normalize(texts)
    img_half = normalize(images)

    def spread(block, dim):
        blocks = [block]
        for _ in range(sizes[dim] - 1):
            blocks.append(shift(blocks[-1], dim, 1))
        return blocks

    def with_cores(blocks):
        out = []
        for block in blocks:
            out.append([block] + [shift(block, 1, by) for by in range(1, cores)])
        return out

    img_targets = [position.reshape(1, rows)] * wide
    txt_targets = spread(lang_order.reshape(1, rows), 3)

    def txt_blocks(block):
        return with_cores(spread(block, 3))

    def img_blocks(block):
        return with_cores(spread(block, 0))

    end = slow - 1
    middle = rows // 2
    txt_line, img_line, txt_sets, img_sets = [txt_half], [img_half], [], []
    for step in range(slow):
        if step == 1:
            block = ring_shift(texts)
            txt_line.append(normalize(block))
        elif step:
            txt_line.append(ring_shift(txt_line[-1]))
        txt_sets.append(txt_blocks(txt_line[-1]))
        if step < end:
            if step == 1:
                block = ring_shift(images)
                img_line.append(normalize(block))
            elif step:
                img_line.append(ring_shift(img_line[-1]))
            img_sets.append(img_blocks(img_line[-1]))
    first = ring_shift(img_line[-1][:middle])
    second = ring_shift(img_line[-1][middle:])
    first_set, second_set = img_blocks(first), img_blocks(second)
    img_own = [cores_of[0] for cores_of in img_sets[0]]
    txt_own = [cores_of[0] for cores_of in txt_sets[0]]

    def image_terms(sums, loss, parts, members, counted):
        blocks, places, pairs = [], [], []
        for step, at in parts:
            if members[0] == 0:
                pairs.append((0, len(blocks)))
            for block in txt_sets[step][at]:
                blocks.append(block)
                places.append((step * fast + at, 0))
        loss_own = range(len(members)) if counted else ()
        own, targets = [img_own[a] for a in members], [img_targets[a] for a in members]
        return terms(own, blocks, places, targets, pairs, ids, settings, sums, loss_own, loss)

    def text_terms(sums, loss, parts, members, counted):
        blocks, places, pairs = [], [], []
        for cores_of, step, at, offset in parts:
            if at == 0:
                pairs += [(a, len(blocks)) for a in range(len(members))]
            for block in cores_of:
                blocks.append(block)
                places.append((step * fast, offset))
        loss_own = range(len(members)) if counted else ()
        own, targets = [txt_own[a] for a in members], [txt_targets[a] for a in members]
        return terms(own, blocks, places, targets, pairs, ids, settings, sums, loss_own, loss)

    img_sums = txt_sums = loss = None
    halves = [(first_set, 0), (second_set, middle)]
    for step in range(end):
        parts = [(step, at) for at in range(fast)]
        img_sums, loss = image_terms(img_sums, loss, parts, range(wide), True)
        parts = [(img_sets[step][at], step, at, 0) for at in range(wide)]
        if step == end - 1:
            parts.append((first_set[0], end, 0, 0))
        txt_sums, loss = text_terms(txt_sums, loss, parts, range(fast), step == 1)
    parts = [(end, at) for at in range(fast)]
    img_far, _ = image_terms(img_sums[1:], None, parts, range(1, wide), False)
    img_near, _ = image_terms(img_sums[:1], None, parts, range(1), False)
    early = [(second_set[0], end, 0, middle)]
    parts = [(half[at], end, at, offset) for at in range(1, wide) for half, offset in halves]
    txt_far, _ = text_terms(txt_sums[1:], None, early, range(1, fast), False)
    txt_far, _ = text_terms(txt_far, None, parts, range(1, fast), False)
    txt_near, _ = text_terms(txt_sums[:1], None, early + parts, range(1), False)
    img_sums, txt_sums = [*img_near, *img_far], [*txt_near, *txt_far]

    addends = [loss]
    for dim in (0, 1, 2, 3):
        by = 1
        while by < sizes[dim]:
            loss = sum(addends[1:], addends[0])
            addends = [loss, exchange(loss, dim, by)]
            by = 2 * by
    total = float(rows * dev_count * group_count)
    img_parts = [img_sums[0]] + [shift(img_sums[a], 0, -a) for a in range(1, wide)]
    txt_parts = [txt_sums[0]] + [shift(txt_sums[a], 3, -a) for a in range(1, fast)]
    image_grad = project(images, settings, img_parts, [], 0.0)
    text_grad, loss = project(texts, settings, txt_parts, addends, 1 / (total * total))
    return (image_grad, text_grad, loss)


def solution(mesh):
    return jax.shard_map(
        per_device,
        mesh=mesh,
        in_specs=(
            P(AXES, None),
            P(AXES, None),
            P(AXES),
            P(AXES),
            P(),
            P(),
        ),
        out_specs=(P(AXES, None), P(AXES, None), P()),
        check_vma=False,
    )
```
